32 devices in a mesh: fsdp: 16 (over z, x, core), heads: 2 (over y).
Axes of the slice: x: 2, y: 2, z: 4, core: 2. Of those that a mesh axis runs over, the one named last changes fastest.
Arguments:
- tokens: bfloat16 [24576, 1280], P(('fsdp', 'heads')), may hold values from -6 to 6
- w_query: bfloat16 [1280, 1280], P('fsdp', 'heads'), may hold values from -0.15625 to 0.15625
- w_key: bfloat16 [1280, 1280], P('fsdp', 'heads'), may hold values from -0.15625 to 0.15625
- w_value: bfloat16 [1280, 1280], P('fsdp', 'heads'), may hold values from -0.15625 to 0.15625
- w_output: bfloat16 [1280, 1280], P('heads', 'fsdp'), may hold values from -0.25 to 0.25
- w_hidden: bfloat16 [1280, 1280], P('fsdp', 'heads'), may hold values from -0.15625 to 0.15625
- bias_hidden: bfloat16 [1280], P(('heads', 'fsdp')), may hold values from -3 to 3
- w_project: bfloat16 [1280, 1280], P('heads', 'fsdp'), may hold values from -0.25 to 0.25
- bias_output: bfloat16 [1280], P(('heads', 'fsdp')), may hold values from -3 to 3
- gain_first: bfloat16 [1280], P(('heads', 'fsdp')), may hold values from 0.099609375 to 1.8984375
- gain_second: bfloat16 [1280], P(('heads', 'fsdp')), may hold values from 0.099609375 to 1.8984375
- lengths: int32 [48, 160], P('fsdp'), may hold values from 1 to 64, 512 in all within a row
- cotangent: bfloat16 [24576, 1280], P(('fsdp', 'heads')), may hold values from -6 to 6
Outputs:
- mixed: bfloat16 [24576, 1280], P(('fsdp', 'heads'))
- grad_tokens: bfloat16 [24576, 1280], P(('fsdp', 'heads'))
- grad_query: float32 [1280, 1280], P('fsdp', 'heads')
- grad_key: float32 [1280, 1280], P('fsdp', 'heads')
- grad_value: float32 [1280, 1280], P('fsdp', 'heads')
- grad_output: float32 [1280, 1280], P('heads', 'fsdp')
- grad_hidden: float32 [1280, 1280], P('fsdp', 'heads')
- grad_hidden_bias: float32 [1280], P(('heads', 'fsdp'))
- grad_project: float32 [1280, 1280], P('heads', 'fsdp')
- grad_output_bias: float32 [1280], P(('heads', 'fsdp'))
- grad_gain_first: float32 [1280], P(('heads', 'fsdp'))
- grad_gain_second: float32 [1280], P(('heads', 'fsdp'))
The draws below stay inside these ranges and needn't reach their ends.
Inputs may be any that keep to these rules, and one draw needn't show every extreme that they name: Each row's 160 lengths sum to 512; every row has a series of exactly 64 patches.
All inputs are finite; a program needn't handle non-finite values.
Results may differ from the reference program's by a relative error of at most 0.022.
Values may be sent and summed in bfloat16 or wider, within the bound.
No kernel may reach another device: no remote copies, remote signals or barrier semaphores. Data moves between devices by JAX's collectives and lax.ppermute only.
A program may use at most 192 MiB of HBM per device.

```python
import math
import jax
import jax.numpy as jnp
import numpy as np
from jax import lax

D = 1280
HEAD_COUNT = 16
HEAD_DIM = 80
FF = 1280
ROW = 512
SERIES = 160
MOST = 64
ROWS = 48
TOKENS = 24576


def block_scale(rng, shape, pieces, smallest, largest):
    factor_of, own = 1.0, jax.random.fold_in(rng, 6)
    for dim, parts in pieces:
        steps = jnp.exp(jax.random.uniform(jax.random.fold_in(own, dim), (parts,), jnp.float32, smallest / len(pieces), largest / len(pieces)))
        factor_of = factor_of * jnp.repeat(steps, shape[dim] // parts).reshape([-1 if axis == dim else 1 for axis in range(len(shape))])
    return factor_of


def split_up(amount, total, reach, slope):
    loads = [(1 << 20) // math.isqrt(rank ** slope) + 1 for rank in range(2, amount + 1)]
    spare, counts = total - reach - (amount - 1), [1] * (amount - 1)
    while spare > 0:
        candidates = [i for i in range(amount - 1) if counts[i] < reach]
        whole, remaining = sum([loads[i] for i in candidates]), spare
        for i in candidates:
            more = min(reach - counts[i], max(1, remaining * loads[i] // whole), spare)
            counts[i] = counts[i] + more
            spare = spare - more
    return np.array([reach] + counts)


def uneven(rng, number_of, total, most, skew):
    if number_of == 2:
        one = jax.random.randint(rng, (), max(1, total - most), min(most, total - 1) + 1)
        return jnp.stack([one, total - one])
    sizes = jnp.asarray(split_up(number_of, total, most, skew), jnp.int32)
    couples = (number_of - 1) // 2
    giver, taker = sizes[1:1 + 2 * couples:2], sizes[2:2 + 2 * couples:2]
    margin = jnp.minimum(giver - 1, most - taker)
    passed = jax.random.randint(jax.random.fold_in(rng, 1), (couples,), 0, 1 << 20) % (margin + 1)
    sizes = sizes.at[1:1 + 2 * couples:2].set(giver - passed).at[2:2 + 2 * couples:2].set(taker + passed)
    return sizes[jax.random.permutation(jax.random.fold_in(rng, 2), number_of)]


def noise(stream_key, extent, spread, bound, shards=(), held_as=jnp.bfloat16):
    values = spread * jax.random.normal(stream_key, extent, jnp.float32)
    if shards:
        values = values * block_scale(stream_key, extent, shards, -0.22, 0.18)
    return jnp.clip(values, -bound, bound).astype(held_as)


def setup_inputs(seed: int = 0) -> dict:
    key_of = jax.random.split(jax.random.key(seed), 14)
    tokens = noise(key_of[0], (TOKENS, D), 1.0, 6.0, ((0, 32),))
    w_query = noise(key_of[1], (D, D), D ** -0.5, 0.15625, ((0, 16), (1, 2)))
    w_key = noise(key_of[2], (D, D), D ** -0.5, 0.15625, ((0, 16), (1, 2)))
    w_value = noise(key_of[3], (D, D), D ** -0.5, 0.15625, ((0, 16), (1, 2)))
    w_output = noise(key_of[4], (D, D), (D // 2) ** -0.5, 0.25, ((0, 2), (1, 16)))
    w_hidden = noise(key_of[5], (D, FF), D ** -0.5, 0.15625, ((0, 16), (1, 2)))
    bias_hidden = noise(key_of[6], (FF,), 0.5, 3.0, ((0, 32),))
    w_project = noise(key_of[7], (FF, D), (FF // 2) ** -0.5, 0.25, ((0, 2), (1, 16)))
    bias_output = noise(key_of[8], (D,), 0.5, 3.0, ((0, 32),))
    gain_first = jnp.clip(1.0 + 0.18 * jax.random.normal(key_of[9], (D,), jnp.float32), 0.099609375, 1.8984375).astype(jnp.bfloat16)
    gain_second = jnp.clip(1.0 + 0.18 * jax.random.normal(key_of[10], (D,), jnp.float32), 0.099609375, 1.8984375).astype(jnp.bfloat16)
    lengths = jax.vmap(lambda own: uneven(own, SERIES, ROW, MOST, 2))(jax.random.split(key_of[11], ROWS)).reshape((ROWS, SERIES)).astype(jnp.int32)
    cotangent = noise(key_of[12], (TOKENS, D), 1.0, 6.0, ((0, 32),))
    return {"tokens": tokens, "w_query": w_query, "w_key": w_key, "w_value": w_value, "w_output": w_output, "w_hidden": w_hidden, "bias_hidden": bias_hidden, "w_project": w_project, "bias_output": bias_output, "gain_first": gain_first, "gain_second": gain_second, "lengths": lengths, "cotangent": cotangent}


EPS = 1e-06
NEG = -1e+30
THETA = 10000.0
HIGH = lax.Precision.HIGHEST

@jax.custom_vjp
def low(v):
    return lax.optimization_barrier(v.astype(jnp.bfloat16)).astype(jnp.float32)

@jax.custom_vjp
def low_back(v):
    return v

def low_keep(v):
    return (low(v), None)

def low_pass(kept, grad):
    return (grad,)

def back_keep(v):
    return (v, None)

def back_low(kept, grad):
    return (low(grad),)
low.defvjp(low_keep, low_pass)
low_back.defvjp(back_keep, back_low)

def tables(lengths_row):
    ends = jnp.cumsum(lengths_row, dtype=jnp.int32)
    place = jnp.arange(ROW, dtype=jnp.int32)
    done = ends[None, :] <= place[:, None]
    series = lax.optimization_barrier(jnp.sum(done.astype(jnp.int32), axis=1, dtype=jnp.int32))
    offset = lax.optimization_barrier(jnp.sum(jnp.where(done, lengths_row[None, :], 0), axis=1, dtype=jnp.int32))
    position = (place - offset).astype(jnp.float32)
    allowed = (series[:, None] == series[None, :]) & (place[None, :] <= place[:, None])
    half = HEAD_DIM // 2
    freq = jnp.exp(-jnp.arange(half, dtype=jnp.float32) * (2.0 * math.log(THETA) / HEAD_DIM))
    angle = position[:, None] * freq[None, :]
    return (allowed, jnp.cos(angle), jnp.sin(angle))

def turn(vectors, cosine, sine):
    half = vectors.shape[-1] // 2
    first = vectors[..., :half]
    second = vectors[..., half:]
    return jnp.concatenate([first * cosine - second * sine, second * cosine + first * sine], axis=-1)

def layer(source, w_query, w_key, w_value, w_output, w_hidden, bias_hidden, w_project, bias_output, gain_first, gain_second, allowed, cosine, sine):
    width = source.shape[1]
    factor_one = lax.rsqrt(lax.optimization_barrier(jnp.mean(source * source, axis=1, keepdims=True)) + EPS)
    normed = low(source * factor_one * gain_first)

    def split_heads(weight):
        return jnp.dot(normed, weight, precision=HIGH).reshape(ROW, HEAD_COUNT, HEAD_DIM)
    cos_heads = cosine[:, None, :]
    sin_heads = sine[:, None, :]
    queries = low(turn(low_back(split_heads(w_query)), cos_heads, sin_heads))
    keys = low(turn(low_back(split_heads(w_key)), cos_heads, sin_heads))
    values = low(low_back(split_heads(w_value)))
    scores = low_back(jnp.einsum('qhd,khd->hqk', queries, keys, precision=HIGH) * HEAD_DIM ** (-0.5))
    scores = jnp.where(allowed[None], scores, NEG)
    weights = low(jax.nn.softmax(scores, axis=-1))
    heads_out = jnp.einsum('hqk,khd->qhd', weights, values, precision=HIGH).reshape(ROW, width)
    attended = low(low_back(heads_out))
    resid = source + low_back(jnp.dot(attended, w_output, precision=HIGH))
    factor_two = lax.rsqrt(lax.optimization_barrier(jnp.mean(resid * resid, axis=1, keepdims=True)) + EPS)
    second = low(resid * factor_two * gain_second)
    hidden = low_back(jnp.dot(second, w_hidden, precision=HIGH) + bias_hidden)
    active = low(jax.nn.gelu(hidden, approximate=True))
    return resid + low_back(jnp.dot(active, w_project, precision=HIGH)) + bias_output

def reference(tokens, w_query, w_key, w_value, w_output, w_hidden, bias_hidden, w_project, bias_output, gain_first, gain_second, lengths, cotangent):
    params = tuple((item.astype(jnp.float32) for item in (w_query, w_key, w_value, w_output, w_hidden, bias_hidden, w_project, bias_output, gain_first, gain_second)))
    count = tokens.shape[0] // ROW
    inputs = tokens.astype(jnp.float32).reshape(count, ROW, tokens.shape[1])
    grads_in = cotangent.astype(jnp.float32).reshape(count, ROW, tokens.shape[1])

    def step(carry, item):
        rows, grad_rows, lens = item
        allowed, cosine, sine = tables(lens)

        def run(rows, *weights):
            return layer(rows, *weights, allowed, cosine, sine)
        result, pull = jax.vjp(run, rows, *params)
        grads = pull(grad_rows)
        carry = tuple((left + right for left, right in zip(carry, grads[1:])))
        return (carry, (result.astype(jnp.bfloat16), grads[0].astype(jnp.bfloat16)))
    start = tuple((jnp.zeros_like(item) for item in params))
    totals, (results, input_grads) = lax.scan(step, start, (inputs, grads_in, lengths))
    return (results.reshape(tokens.shape), input_grads.reshape(tokens.shape), totals[0], totals[1], totals[2], totals[3], totals[4], totals[5], totals[6], totals[7], totals[8], totals[9])
```

```python
from functools import partial
import math

import jax
import jax.numpy as jnp
from jax import lax
from jax.experimental import pallas as pl
from jax.experimental.pallas import tpu as pltpu
from jax.sharding import PartitionSpec as P

HEAD_DIM = 80
ROW = 512
MOST = 64
EPS = 1e-06
NEG = -1e30
THETA = 10000.0
ALL = ("fsdp", "heads")
BF = jnp.bfloat16
F32 = jnp.float32
VMEM_LIMIT = 60 * 1024 * 1024


def bits_of(n):
    return n.bit_length() - 1


def reverse_bits(values, count):
    out = 0
    for bit in range(count):
        out = out | (((values >> bit) & 1) << (count - 1 - bit))
    return out


class Links:
    def __init__(self, fsdp, heads):
        self.count = fsdp * heads
        self.hbits, self.fbits = bits_of(heads), bits_of(fsdp)
        desc = list(range(self.hbits + self.fbits - 1, self.hbits - 1, -1))
        self.z, self.x, self.core = desc[:-2], desc[-2:-1], desc[-1:]
        self.y = list(range(self.hbits - 1, -1, -1))

    def swap(self, value, bit):
        pairs = [(d, d ^ (1 << bit)) for d in range(self.count)]
        return lax.ppermute(value, ALL, pairs)

    def join(self, value, bit, axis):
        return jnp.concatenate([value, self.swap(value, bit)], axis=axis)

    def order(self, first):
        x = [(b, 0) for b in self.x]
        y = [(b, 1) for b in self.y]
        return x + y if first == "x" else y + x

    def gather_pair(self, left, right):
        both = jnp.stack([left, right])
        for bit in self.z:
            both = self.join(both, bit, 1)
        out = []
        for value, first in ((both[0], "x"), (both[1], "y")):
            for bit, axis in self.order(first):
                value = self.join(value, bit, axis)
            for bit in self.core:
                value = self.join(value, bit, 0)
            out.append(value)
        return out

    def fold(self, value, bit, axis):
        half = value.shape[axis] // 2
        keep = lax.slice_in_dim(value, 0, half, axis=axis)
        send = lax.slice_in_dim(value, half, 2 * half, axis=axis)
        return keep + self.swap(send.astype(BF), bit).astype(F32)

    def scatter_pair(self, left, right):
        out = []
        for value, first in ((left, "y"), (right, "x")):
            for bit in self.core:
                value = self.fold(value, bit, 0)
            other = "x" if first == "y" else "y"
            for bit, axis in reversed(self.order(other)):
                value = self.fold(value, bit, axis)
            out.append(value)
        both = jnp.stack(out)
        for bit in reversed(self.z):
            both = self.fold(both, bit, 1)
        return both[0], both[1]


def flip_kernel(parts, source, x_ref, out_ref, held):
    size = x_ref.shape[1] // parts
    held[...] = x_ref[...].astype(F32).T
    for part in range(parts):
        start = pl.multiple_of(source[part] * size, 8)
        out_ref[part * size : (part + 1) * size, :] = held[pl.ds(start, size), :]


def flip(value, source, parts):
    rows, cols = value.shape
    return pl.pallas_call(
        partial(flip_kernel, parts),
        out_shape=jax.ShapeDtypeStruct((cols, rows), F32),
        in_specs=[
            pl.BlockSpec(memory_space=pltpu.SMEM),
            pl.BlockSpec(memory_space=pltpu.VMEM),
        ],
        out_specs=pl.BlockSpec(memory_space=pltpu.VMEM),
        scratch_shapes=[pltpu.VMEM((cols, rows), F32)],
        compiler_params=pltpu.CompilerParams(vmem_limit_bytes=VMEM_LIMIT),
    )(source, value)


def unflip_kernel(parts, source, x_ref, out_ref, held):
    size = x_ref.shape[0] // parts
    for part in range(parts):
        start = pl.multiple_of(source[part] * size, 8)
        held[pl.ds(start, size), :] = x_ref[part * size : (part + 1) * size, :]
    out_ref[...] = held[...].T.astype(BF)


def unflip(value, source, parts):
    rows, cols = value.shape
    return pl.pallas_call(
        partial(unflip_kernel, parts),
        out_shape=jax.ShapeDtypeStruct((cols, rows), BF),
        in_specs=[
            pl.BlockSpec(memory_space=pltpu.SMEM),
            pl.BlockSpec(memory_space=pltpu.VMEM),
        ],
        out_specs=pl.BlockSpec(memory_space=pltpu.VMEM),
        scratch_shapes=[pltpu.VMEM((rows, cols), F32)],
        compiler_params=pltpu.CompilerParams(vmem_limit_bytes=VMEM_LIMIT),
    )(source, value)


def turn(vectors, cosine, sine):
    half = vectors.shape[0] // 2
    first, second = vectors[:half], vectors[half:]
    return jnp.concatenate([first * cosine - second * sine, second * cosine + first * sine], axis=0)


def dot_tn(left, right):
    return lax.dot_general(left, right, (((0,), (0,)), ((), ())), preferred_element_type=F32)


def dot_nn(left, right):
    return lax.dot_general(left, right, (((1,), (0,)), ((), ())), preferred_element_type=F32)


def dot_nt(left, right):
    return lax.dot_general(left, right, (((1,), (1,)), ((), ())), preferred_element_type=F32)


def fill_bias(begin_ref, bias_ref, halo, block, window):
    blocks = bias_ref.shape[0]
    for b in range(blocks):
        low = b * block
        key = lax.broadcasted_iota(jnp.int32, (window, block), 0) + low
        query = lax.broadcasted_iota(jnp.int32, (window, block), 1) + (halo + low)
        begin = begin_ref[0:1, low : low + block]
        bias_ref[b] = jnp.where((key >= begin) & (key <= query), 0.0, NEG)


def attend_kernel(halo, block, q_ref, k_ref, v_ref, cos_ref, sin_ref, begin_ref,
                  qr_ref, kr_ref, vr_ref, att_ref, log_ref, bias_ref):
    own = q_ref.shape[1]
    window = halo + block
    scale = HEAD_DIM ** (-0.5)

    @pl.when(pl.program_id(0) == 0)
    def _():
        fill_bias(begin_ref, bias_ref, halo, block, window)

    cosine, sine = cos_ref[...], sin_ref[...]
    q = turn(q_ref[...], cosine[:, halo:], sine[:, halo:]).astype(BF)
    k = turn(k_ref[...], cosine, sine).astype(BF)
    v = v_ref[...].astype(BF)
    qr_ref[...] = q
    kr_ref[...] = k
    vr_ref[...] = v
    for b in range(own // block):
        low = b * block
        qb, kb, vb = q[:, low : low + block], k[:, low : low + window], v[:, low : low + window]
        scores = dot_tn(kb, qb) * scale + bias_ref[b]
        peak = jnp.max(scores, axis=0, keepdims=True)
        expo = jnp.exp(scores - peak)
        total = jnp.sum(expo, axis=0, keepdims=True)
        weights = (expo / total).astype(BF)
        att_ref[:, low : low + block] = dot_nn(vb, weights).astype(BF)
        log_ref[0, :, low : low + block] = peak + jnp.log(total)


def attend(q, k, v, cosine, sine, begin, halo, block):
    inner, own = q.shape
    total = halo + own
    heads = inner // HEAD_DIM
    per = lambda n: pl.BlockSpec((HEAD_DIM, n), lambda i: (i, 0))
    full = lambda a: pl.BlockSpec(a.shape, lambda i: (0, 0))
    return pl.pallas_call(
        partial(attend_kernel, halo, block),
        grid=(heads,),
        out_shape=(
            jax.ShapeDtypeStruct((inner, own), BF),
            jax.ShapeDtypeStruct((inner, total), BF),
            jax.ShapeDtypeStruct((inner, total), BF),
            jax.ShapeDtypeStruct((inner, own), BF),
            jax.ShapeDtypeStruct((heads, 1, own), F32),
        ),
        in_specs=[per(own), per(total), per(total), full(cosine), full(sine), full(begin)],
        out_specs=(per(own), per(total), per(total), per(own), pl.BlockSpec((1, 1, own), lambda i: (i, 0, 0))),
        scratch_shapes=[pltpu.VMEM((own // block, halo + block, block), F32)],
        compiler_params=pltpu.CompilerParams(vmem_limit_bytes=VMEM_LIMIT),
    )(q, k, v, cosine, sine, begin)


def attend_back_kernel(halo, block, q_ref, k_ref, v_ref, g_ref, log_ref, cos_ref, sin_ref, begin_ref,
                       dq_ref, dk_ref, dv_ref, dkh_ref, dvh_ref, bias_ref, dk_sum, dv_sum):
    own = q_ref.shape[1]
    window = halo + block
    scale = HEAD_DIM ** (-0.5)

    @pl.when(pl.program_id(0) == 0)
    def _():
        fill_bias(begin_ref, bias_ref, halo, block, window)

    cosine, sine = cos_ref[...], sin_ref[...]
    dk_sum[...] = jnp.zeros_like(dk_sum)
    dv_sum[...] = jnp.zeros_like(dv_sum)
    for b in range(own // block):
        low = b * block
        mine, seen = slice(low, low + block), slice(low, low + window)
        qb, kb, vb, gb = q_ref[:, mine], k_ref[:, seen], v_ref[:, seen], g_ref[:, mine]
        scores = dot_tn(kb, qb) * scale + bias_ref[b]
        probs = jnp.exp(scores - log_ref[0, :, mine])
        dv_sum[:, seen] += dot_nt(gb, probs.astype(BF))
        grad_probs = dot_tn(vb, gb)
        inner = jnp.sum(probs * grad_probs, axis=0, keepdims=True)
        grad_scores = (probs * (grad_probs - inner)).astype(BF)
        dq = dot_nn(kb, grad_scores) * scale
        dk_sum[:, seen] += dot_nt(qb, grad_scores)
        own_seen = slice(halo + low, halo + low + block)
        dq_ref[:, mine] = turn(dq, cosine[:, own_seen], -sine[:, own_seen]).astype(BF)
    dk = turn(dk_sum[...] * scale, cosine, -sine).astype(BF)
    dk_ref[...] = dk[:, halo:]
    dkh_ref[...] = dk[:, :halo]
    dv = dv_sum[...].astype(BF)
    dv_ref[...] = dv[:, halo:]
    dvh_ref[...] = dv[:, :halo]


def attend_back(q, k, v, g, logs, cosine, sine, begin, halo, block):
    inner, own = q.shape
    total = halo + own
    heads = inner // HEAD_DIM
    per = lambda n: pl.BlockSpec((HEAD_DIM, n), lambda i: (i, 0))
    full = lambda a: pl.BlockSpec(a.shape, lambda i: (0, 0))
    return pl.pallas_call(
        partial(attend_back_kernel, halo, block),
        grid=(heads,),
        out_shape=tuple(jax.ShapeDtypeStruct((inner, n), BF) for n in (own, own, own, halo, halo)),
        in_specs=[per(own), per(total), per(total), per(own), pl.BlockSpec((1, 1, own), lambda i: (i, 0, 0)),
                  full(cosine), full(sine), full(begin)],
        out_specs=tuple(per(n) for n in (own, own, own, halo, halo)),
        scratch_shapes=[
            pltpu.VMEM((own // block, halo + block, block), F32),
            pltpu.VMEM((HEAD_DIM, total), F32),
            pltpu.VMEM((HEAD_DIM, total), F32),
        ],
        compiler_params=pltpu.CompilerParams(vmem_limit_bytes=VMEM_LIMIT),
    )(q, k, v, g, logs, cosine, sine, begin)


def norm_back(grad_norm, source, factor, gain):
    scaled = gain * grad_norm
    inner = jnp.mean(scaled * source, axis=0, keepdims=True)
    grad_source = factor * scaled - source * (factor * factor * factor) * inner
    return grad_source, jnp.sum(grad_norm * source * factor, axis=1)


def local(fsdp, heads, tokens, w_query, w_key, w_value, w_output, w_hidden, bias_hidden, w_project,
          bias_output, gain_first, gain_second, lengths, cotangent):
    links = Links(fsdp, heads)
    own, width = tokens.shape
    inner = w_query.shape[1] * heads
    f_at, h_at = lax.axis_index("fsdp"), lax.axis_index("heads")
    me = f_at * heads + h_at
    halo = 128 if own % 128 == 0 else MOST
    block = 256 if own % 256 == 0 else own
    source = f_at ^ reverse_bits(jnp.arange(fsdp, dtype=jnp.int32), links.fbits)
    back = reverse_bits(jnp.arange(fsdp, dtype=jnp.int32) ^ f_at, links.fbits)
    inner_source = h_at ^ reverse_bits(jnp.arange(heads, dtype=jnp.int32), links.hbits)
    inner_back = reverse_bits(jnp.arange(heads, dtype=jnp.int32) ^ h_at, links.hbits)

    small = jnp.concatenate([bias_hidden, bias_output, gain_first, gain_second])[None]
    piece = bias_hidden.shape[0]
    for bit in range(links.hbits + links.fbits):
        small = links.join(small, bit, 0)
    small = small[me ^ jnp.arange(fsdp * heads, dtype=jnp.int32)].astype(F32)
    small = small.reshape(fsdp, heads, 4, piece).transpose(2, 1, 0, 3).reshape(4, -1)

    def to_rel(vector):
        return vector.reshape(fsdp, -1)[source].reshape(-1, 1)

    shift_hidden = small[0].reshape(heads, -1)[inner_source].reshape(-1, 1)
    shift_output, gain_one, gain_two = to_rel(small[1]), to_rel(small[2]), to_rel(small[3])

    before = lax.ppermute(tokens[own - MOST :], "heads", [(i, i + 1) for i in range(heads - 1)])
    seen = jnp.concatenate([jnp.zeros((halo - MOST, width), tokens.dtype), before, tokens], axis=0)

    ends = jnp.cumsum(lengths, axis=1, dtype=jnp.int32)
    place = jnp.arange(ROW, dtype=jnp.int32)
    done = ends[:, None, :] <= place[None, :, None]
    offset = jnp.sum(jnp.where(done, lengths[:, None, :], 0), axis=2, dtype=jnp.int32)
    spot = (place[None] - offset).reshape(-1)
    spot = jnp.concatenate([jnp.zeros((halo,), jnp.int32), spot])
    spot = lax.dynamic_slice_in_dim(spot, h_at * own, halo + own, 0)
    begin = (jnp.arange(own, dtype=jnp.int32) + halo - spot[halo:])[None]
    half = HEAD_DIM // 2
    freq = jnp.exp(-jnp.arange(half, dtype=F32) * (2.0 * math.log(THETA) / HEAD_DIM))
    angle = freq[:, None] * spot.astype(F32)[None]
    cosine, sine = jnp.cos(angle), jnp.sin(angle)

    full_query, full_key = links.gather_pair(w_query, w_key)
    full_value, full_output = links.gather_pair(w_value, w_output.T)
    full_hidden, full_project = links.gather_pair(w_hidden, w_project.T)

    x = flip(seen, source, fsdp)
    cot = flip(cotangent, source, fsdp)
    factor_one = lax.rsqrt(jnp.mean(x * x, axis=0, keepdims=True) + EPS)
    normed = (x * factor_one * gain_one).astype(BF)
    normed_own = normed[:, halo:]
    source_own = x[:, halo:]
    factor_own = factor_one[:, halo:]

    q = dot_tn(full_query, normed_own)
    k = dot_tn(full_key, normed)
    v = dot_tn(full_value, normed)
    q, k, v, attended, logs = attend(q, k, v, cosine, sine, begin, halo, block)
    resid = source_own + dot_nn(full_output, attended)
    factor_two = lax.rsqrt(jnp.mean(resid * resid, axis=0, keepdims=True) + EPS)
    second = (resid * factor_two * gain_two).astype(BF)
    hidden = dot_tn(full_hidden, second) + shift_hidden
    active_full, pull = jax.vjp(partial(jax.nn.gelu, approximate=True), hidden)
    active = active_full.astype(BF)
    cot_low = cot.astype(BF)
    grad_project = dot_nt(cot_low, active)
    mixed = resid + dot_nn(full_project, active) + shift_output

    grad_output_bias = jnp.sum(cot, axis=1)
    grad_pre = pull(dot_tn(full_project, cot_low))[0].astype(BF)
    grad_hidden_bias = jnp.sum(grad_pre.astype(F32), axis=1)
    grad_hidden = dot_nt(second, grad_pre)
    grad_second = dot_nn(full_hidden, grad_pre)
    resid_term, grad_gain_second = norm_back(grad_second, resid, factor_two, gain_two)
    grad_resid = cot + resid_term
    grad_branch = grad_resid.astype(BF)
    grad_output = dot_nt(grad_branch, attended)
    grad_attended = dot_tn(full_output, grad_branch).astype(BF)
    dq, dk, dv, dk_halo, dv_halo = attend_back(q, k, v, grad_attended, logs, cosine, sine, begin, halo, block)
    extra = jnp.concatenate([dk_halo[:, halo - MOST :], dv_halo[:, halo - MOST :]], axis=0)
    extra = lax.ppermute(extra, "heads", [(i + 1, i) for i in range(heads - 1)]).astype(F32)
    shuffle = reverse_bits((h_at + 1) ^ h_at, links.hbits) ^ jnp.arange(heads, dtype=jnp.int32)
    groups = extra.reshape(2, heads, -1, MOST)
    extra = (groups[:, ::-1] if heads == 2 else groups[:, shuffle]).reshape(extra.shape)
    tail = jnp.pad(extra, ((0, 0), (own - MOST, 0)))
    dk = (dk.astype(F32) + tail[:inner]).astype(BF)
    dv = (dv.astype(F32) + tail[inner:]).astype(BF)
    grad_query = dot_nt(normed_own, dq)
    grad_key = dot_nt(normed_own, dk)
    grad_value = dot_nt(normed_own, dv)
    grad_normed = dot_nn(full_query, dq) + dot_nn(full_key, dk) + dot_nn(full_value, dv)
    source_term, grad_gain_first = norm_back(grad_normed, source_own, factor_own, gain_one)
    grad_tokens = grad_resid + source_term

    out_project, out_hidden = links.scatter_pair(grad_project, grad_hidden)
    out_output, out_value = links.scatter_pair(grad_output, grad_value)
    out_query, out_key = links.scatter_pair(grad_query, grad_key)

    def to_abs(vector):
        return vector.reshape(fsdp, -1)[back].reshape(-1)

    vecs = jnp.stack([
        grad_hidden_bias.reshape(heads, -1)[inner_back].reshape(-1),
        to_abs(grad_output_bias), to_abs(grad_gain_first), to_abs(grad_gain_second),
    ])
    vecs = vecs.reshape(4, heads, fsdp, piece).transpose(2, 1, 0, 3).reshape(fsdp * heads, 4 * piece)
    vecs = vecs[me ^ jnp.arange(fsdp * heads, dtype=jnp.int32)]
    for bit in reversed(range(links.hbits + links.fbits)):
        rows = vecs.shape[0] // 2
        vecs = vecs[:rows] + links.swap(vecs[rows:], bit)
    vecs = vecs.reshape(4, piece)

    return (
        unflip(mixed, source, fsdp),
        unflip(grad_tokens, source, fsdp),
        out_query, out_key, out_value, out_output.T, out_hidden,
        vecs[0], out_project.T, vecs[1], vecs[2], vecs[3],
    )


def solution(mesh):
    fsdp, heads = mesh.shape["fsdp"], mesh.shape["heads"]
    rows, cols = P("fsdp", "heads"), P("heads", "fsdp")
    tokens, vector = P(("fsdp", "heads"), None), P(("heads", "fsdp"))
    return jax.shard_map(
        partial(local, fsdp, heads),
        mesh=mesh,
        in_specs=(tokens, rows, rows, rows, cols, rows, vector, cols, vector, vector, vector, P("fsdp", None), tokens),
        out_specs=(tokens, tokens, rows, rows, rows, cols, rows, vector, cols, vector, vector, vector),
        check_vma=False,
    )
```

```python
from functools import partial
import math

import jax
import jax.numpy as jnp
from jax import lax
from jax.experimental import pallas as pl
from jax.experimental.pallas import tpu as pltpu
from jax.sharding import PartitionSpec as P

HEAD_DIM = 80
ROW = 512
MOST = 64
EPS = 1e-06
NEG = -1e30
THETA = 10000.0
ALL = ("fsdp", "heads")
BF = jnp.bfloat16
F32 = jnp.float32
MIB = 1024 * 1024


def bits_of(n):
    return n.bit_length() - 1


def reverse_bits(values, count):
    out = 0
    for bit in range(count):
        out = out | (((values >> bit) & 1) << (count - 1 - bit))
    return out


class Lane:
    def __init__(self, steps):
        self.steps, self.result, self.pending = steps, None, []
        self.push(None)

    def push(self, values):
        try:
            self.pending = list(self.steps.send(values))
        except StopIteration as stop:
            self.steps, self.pending, self.result = None, [], stop.value

    @property
    def open(self):
        return self.steps is not None


def tick(lanes, values=()):
    lanes = [lane for lane in lanes if lane.open]
    counts = [len(lane.pending) for lane in lanes]
    flat = [v for lane in lanes for v in lane.pending] + list(values)
    flat = list(lax.optimization_barrier(tuple(flat)))
    at = 0
    for lane, count in zip(lanes, counts):
        lane.push(flat[at : at + count])
        at += count
    return flat[at:]


def finish(lane):
    while lane.open:
        tick([lane])
    return lane.result


class Links:
    def __init__(self, fsdp, heads, rows):
        self.count = fsdp * heads
        self.hbits, self.fbits = bits_of(heads), bits_of(fsdp)
        desc = list(range(self.hbits + self.fbits - 1, self.hbits - 1, -1))
        self.z, self.x, self.core = desc[:-2], desc[-2], desc[-1]
        self.y = list(range(self.hbits - 1, -1, -1))
        self.shift = {bit: (rows << i, 0) for i, bit in enumerate(desc)}
        self.shift.update({bit: (0, 1 << i) for i, bit in enumerate(self.y)})

    def swap(self, value, bit):
        pairs = [(d, d ^ (1 << bit)) for d in range(self.count)]
        return lax.ppermute(value, ALL, pairs)

    def moved(self, places, bit):
        row, group = self.shift[bit]
        return [(r + row, g + group) for r, g in places]

    def spread(self, value, places, bits):
        for bit in bits:
            value, other = yield [value, self.swap(value, bit)]
            value = jnp.concatenate([value, other], axis=1)
            places = [p + self.moved(p, bit) for p in places]
        return value, places

    def plane(self, value, places, bits):
        for bit in bits[:-1]:
            value, other = yield [value, self.swap(value, bit)]
            value = jnp.concatenate([value, other], axis=0)
            places = places + self.moved(places, bit)
        value, other, far = yield [value, self.swap(value, bits[-1]), self.swap(value, self.core)]
        last = self.moved(places, bits[-1])
        far_other = self.swap(other, self.core)
        pieces = [(value, places), (other, last), (far, self.moved(places, self.core)),
                  (far_other, self.moved(last, self.core))]
        pieces = [self.packed(v, p) for v, p in pieces]
        if value.shape[2] % 128:
            return self.whole(pieces)
        return pieces

    def packed(self, value, places):
        n, rows, cols = value.shape
        run = 1
        while run * 2 <= n and all(
            places[i + j] == (places[i][0] + j * rows, places[i][1])
            for i in range(0, n, run * 2) for j in range(run * 2)
        ):
            run *= 2
        return value.reshape(n // run, rows * run, cols), places[::run]

    def whole(self, pieces):
        cols = pieces[0][0].shape[2]
        rows = max(r + v.shape[1] for v, places in pieces for r, g in places)
        groups = max(g + 1 for v, places in pieces for r, g in places)
        full = jnp.zeros((rows, groups * cols), BF)
        for v, places in pieces:
            for i, (r, g) in enumerate(places):
                full = lax.dynamic_update_slice(full, v[i], (r, g * cols))
        return [(full[None], [(0, 0)])]

    def halves(self, value, axis):
        half = value.shape[axis] // 2
        return (lax.slice_in_dim(value, 0, half, axis=axis), lax.slice_in_dim(value, half, 2 * half, axis=axis))

    def add(self, keep, received):
        return (keep.astype(F32) + received.astype(F32)).astype(BF)

    def fold_plane(self, keep, send, first):
        keep, received = yield [keep, self.swap(send, self.core)]
        value = self.add(keep, received)
        steps = [(self.x, 0)] + [(b, 1) for b in reversed(self.y)]
        if first == "y":
            steps = steps[1:] + steps[:1]
        for bit, axis in steps:
            keep, send = self.halves(value, axis)
            keep, received = yield [keep, self.swap(send, bit)]
            value = self.add(keep, received)
        return value

    def fold_group(self, values):
        both = jnp.stack(values)
        for bit in reversed(self.z):
            keep, send = self.halves(both, 1)
            keep, received = yield [keep, self.swap(send, bit)]
            both = self.add(keep, received)
        return [both[i].astype(F32) for i in range(len(values))]

    def collect(self, value, bits):
        for bit in bits:
            value, other = yield [value, self.swap(value, bit)]
            value = jnp.concatenate([value, other], axis=0)
        return value


def work(us):
    return pl.CostEstimate(flops=int(us * 0.55e9), bytes_accessed=1 << 20, transcendentals=0)


def dot_tn(left, right):
    return lax.dot_general(left, right, (((0,), (0,)), ((), ())), preferred_element_type=F32)


def dot_nn(left, right):
    return lax.dot_general(left, right, (((1,), (0,)), ((), ())), preferred_element_type=F32)


def dot_nt(left, right):
    return lax.dot_general(left, right, (((1,), (1,)), ((), ())), preferred_element_type=F32)


def run(body, name, us, mib, outs, weights, args, scratch=(), smem=()):
    plans = [[places for _, places in pieces] for pieces in weights]
    arrays = [v for pieces in weights for v, _ in pieces]
    copies = [sum(v.shape[0] for v, _ in pieces) for pieces in weights]
    shapes = []
    for pieces in weights:
        rows = max(r + v.shape[1] for v, places in pieces for r, g in places)
        groups = max(g + 1 for v, places in pieces for r, g in places)
        shapes.append((rows, groups * pieces[0][0].shape[2]))
    n_s, n_a, n_in, n_w, n_out = len(smem), len(arrays), len(args), len(weights), len(outs)

    def kernel(*refs):
        at = 0
        s_refs, at = refs[at : at + n_s], at + n_s
        a_refs, at = refs[at : at + n_a], at + n_a
        in_refs, at = refs[at : at + n_in], at + n_in
        o_refs, at = refs[at : at + n_out], at + n_out
        w_refs, at = refs[at : at + n_w], at + n_w
        sems, at = refs[at : at + n_w], at + n_w
        started = []
        k = 0
        for w, plan in enumerate(plans):
            n = 0
            mine = []
            for places in plan:
                piece = a_refs[k]
                k += 1
                _, rows, cols = piece.shape
                for i, (row, group) in enumerate(places):
                    target = w_refs[w].at[row : row + rows, group * cols : (group + 1) * cols]
                    mine.append(pltpu.make_async_copy(piece.at[i], target, sems[w].at[n]))
                    n += 1
            started.append(mine)
        for mine in started:
            for copy in mine:
                copy.start()

        def ready(w):
            for copy in started[w]:
                copy.wait()
            return w_refs[w]

        body(s_refs, ready, in_refs, o_refs, refs[at:])

    vmem, anywhere = pl.BlockSpec(memory_space=pltpu.VMEM), pl.BlockSpec(memory_space=pl.ANY)
    out = pl.pallas_call(
        kernel,
        name=name,
        out_shape=tuple(jax.ShapeDtypeStruct(s, d) for s, d in outs),
        in_specs=[pl.BlockSpec(memory_space=pltpu.SMEM)] * n_s + [anywhere] * n_a + [vmem] * n_in,
        out_specs=(vmem,) * n_out,
        scratch_shapes=[pltpu.VMEM(s, BF) for s in shapes]
        + [pltpu.SemaphoreType.DMA((n,)) for n in copies] + list(scratch),
        compiler_params=pltpu.CompilerParams(vmem_limit_bytes=mib * MIB),
        cost_estimate=work(us),
    )(*smem, *arrays, *args)
    return out


def over_tokens(own, step):
    part = 256 if own % 256 == 0 else own
    if part == own:
        step(0, own)
        return

    @pl.loop(0, own // part)
    def _(i):
        step(pl.multiple_of(i * part, part), part)


def shifted(start, by):
    return start + by if isinstance(start, int) else pl.multiple_of(start + by, 128)


def lane_sums(value):
    count = value.shape[1]
    if count % 128:
        return jnp.pad(jnp.sum(value, axis=1, keepdims=True), ((0, 0), (0, 127)))
    out = value[:, :128]
    for i in range(1, count // 128):
        out = out + value[:, i * 128 : (i + 1) * 128]
    return out


def gradient(left_ref, lanes, right, keep_ref, send_ref):
    rows = keep_ref.shape[0]
    part = 320 if rows % 320 == 0 else rows

    for first, out_ref in ((rows, send_ref), (0, keep_ref)):
        @pl.loop(0, rows // part)
        def _(i):
            at = pl.multiple_of(first + i * part, 16)
            value = dot_nt(left_ref[pl.ds(at, part), lanes], right())
            out_ref[pl.ds(pl.multiple_of(i * part, 16), part), :] = value.astype(BF)


def flip_rows(parts, source, held, put):
    size = held.shape[0] // parts
    for part in range(parts):
        start = pl.multiple_of(source[part] * size, 8)
        put(part * size, size, start)


def flip_norm(seen, source, gain, parts):
    tokens, width = seen.shape

    def body(smem, ready, ins, outs, scratch):
        (source_ref,), (seen_ref, gain_ref), (x_ref, a_ref, r_ref), (held, moved) = smem, ins, outs, scratch
        held[...] = seen_ref[...].astype(F32).T

        def put(row, size, start):
            moved[row : row + size, :] = held[pl.ds(start, size), :]

        flip_rows(parts, source_ref, held, put)
        x = moved[...]
        factor = lax.rsqrt(jnp.mean(x * x, axis=0, keepdims=True) + EPS)
        x_ref[...] = x.astype(BF)
        r_ref[...] = factor
        a_ref[...] = (x * factor * gain_ref[...]).astype(BF)

    return run(body, "flip_norm", 9, 24, [((width, tokens), BF), ((width, tokens), BF), ((1, tokens), F32)],
               [], [seen, gain], [pltpu.VMEM((width, tokens), F32)] * 2, [source])


def flip_sum(value, source, parts):
    tokens, width = value.shape

    def body(smem, ready, ins, outs, scratch):
        (source_ref,), (value_ref,), (x_ref, sum_ref), (held, moved) = smem, ins, outs, scratch
        held[...] = value_ref[...].astype(F32).T

        def put(row, size, start):
            moved[row : row + size, :] = held[pl.ds(start, size), :]

        flip_rows(parts, source_ref, held, put)
        x_ref[...] = moved[...].astype(BF)
        sum_ref[...] = jnp.sum(lane_sums(moved[...]), axis=1, keepdims=True)

    return run(body, "flip_sum", 6, 20, [((width, tokens), BF), ((width, 1), F32)],
               [], [value], [pltpu.VMEM((width, tokens), F32)] * 2, [source])


def turn(vectors, cosine, sine):
    half = vectors.shape[0] // 2
    first, second = vectors[:half], vectors[half:]
    return jnp.concatenate([first * cosine - second * sine, second * cosine + first * sine], axis=0)


def project(weight, a, low, cosine, sine, name):
    width, total = a.shape
    inner = width
    own = total - low if low else None

    def body(smem, ready, ins, outs, scratch):
        (out_ref,) = outs
        a_ref = ins[0]
        w_ref = ready(0)

        def step(start, count, goes):
            value = dot_tn(w_ref[...], a_ref[:, pl.ds(start, count)])
            if cosine is None:
                out_ref[:, pl.ds(goes, count)] = value.astype(BF)
                return
            c, s = ins[1][:, pl.ds(start, count)], ins[2][:, pl.ds(start, count)]
            for head in range(inner // HEAD_DIM):
                rows = slice(head * HEAD_DIM, (head + 1) * HEAD_DIM)
                out_ref[rows, pl.ds(goes, count)] = turn(value[rows], c, s).astype(BF)

        if low:
            over_tokens(own, lambda start, count: step(shifted(start, low), count, start))
        elif total % 256 == 128:
            step(0, 128, 0)
            over_tokens(total - 128, lambda start, count: step(shifted(start, 128), count, shifted(start, 128)))
        else:
            step(0, total, 0)

    args = [a] if cosine is None else [a, cosine, sine]
    (out,) = run(body, name, 5, 18, [((inner, total - low), BF)], [weight], args)
    return out


def fill_bias(begin_ref, bias_ref, halo, block, window):
    for b in range(bias_ref.shape[0]):
        low = b * block
        key = lax.broadcasted_iota(jnp.int32, (window, block), 0) + low
        query = lax.broadcasted_iota(jnp.int32, (window, block), 1) + (halo + low)
        begin = begin_ref[0:1, low : low + block]
        bias_ref[b] = jnp.where((key >= begin) & (key <= query), 0.0, NEG)


def attend_kernel(halo, block, q_ref, k_ref, v_ref, begin_ref, att_ref, log_ref, bias_ref):
    own = q_ref.shape[1]
    window = halo + block
    scale = HEAD_DIM ** (-0.5)

    @pl.when(pl.program_id(0) == 0)
    def _():
        fill_bias(begin_ref, bias_ref, halo, block, window)

    for b in range(own // block):
        low = b * block
        mine, seen = slice(low, low + block), slice(low, low + window)
        scores = dot_tn(k_ref[:, seen], q_ref[:, mine]) * scale + bias_ref[b]
        peak = jnp.max(scores, axis=0, keepdims=True)
        expo = jnp.exp(scores - peak)
        total = jnp.sum(expo, axis=0, keepdims=True)
        weights = (expo * (1.0 / total)).astype(BF)
        att_ref[:, mine] = dot_nn(v_ref[:, seen], weights).astype(BF)
        log_ref[0, :, mine] = peak + jnp.log(total)


def attend(q, k, v, begin, halo, block, first, heads):
    own = q.shape[1]
    total = halo + own
    inner = heads * HEAD_DIM
    per = lambda n: pl.BlockSpec((HEAD_DIM, n), lambda i: (first + i, 0))
    put = pl.BlockSpec((HEAD_DIM, own), lambda i: (i, 0))
    return pl.pallas_call(
        partial(attend_kernel, halo, block),
        grid=(heads,),
        out_shape=(jax.ShapeDtypeStruct((inner, own), BF), jax.ShapeDtypeStruct((heads, 1, own), F32)),
        in_specs=[per(own), per(total), per(total), pl.BlockSpec(begin.shape, lambda i: (0, 0))],
        out_specs=(put, pl.BlockSpec((1, 1, own), lambda i: (i, 0, 0))),
        scratch_shapes=[pltpu.VMEM((own // block, halo + block, block), F32)],
        compiler_params=pltpu.CompilerParams(vmem_limit_bytes=12 * MIB),
        name="attend",
        cost_estimate=work(1.2 * heads),
    )(q, k, v, begin)


def attend_back_kernel(halo, block, q_ref, k_ref, v_ref, g_ref, log_ref, cos_ref, sin_ref, begin_ref,
                       dq_ref, dk_ref, dv_ref, edge_ref, bias_ref, dk_sum, dv_sum):
    own = q_ref.shape[1]
    window = halo + block
    scale = HEAD_DIM ** (-0.5)

    @pl.when(pl.program_id(0) == 0)
    def _():
        fill_bias(begin_ref, bias_ref, halo, block, window)

    cosine, sine = cos_ref[...], sin_ref[...]
    dk_sum[...] = jnp.zeros_like(dk_sum)
    dv_sum[...] = jnp.zeros_like(dv_sum)
    for b in range(own // block):
        low = b * block
        mine, seen = slice(low, low + block), slice(low, low + window)
        qb, kb, vb, gb = q_ref[:, mine], k_ref[:, seen], v_ref[:, seen], g_ref[:, mine]
        scores = dot_tn(kb, qb) * scale + bias_ref[b]
        probs = jnp.exp(scores - log_ref[0, :, mine])
        dv_sum[:, seen] += dot_nt(gb, probs.astype(BF))
        grad_probs = dot_tn(vb, gb)
        inner = jnp.sum(probs * grad_probs, axis=0, keepdims=True)
        grad_scores = (probs * (grad_probs - inner)).astype(BF)
        dq = dot_nn(kb, grad_scores) * scale
        dk_sum[:, seen] += dot_nt(qb, grad_scores)
        own_seen = slice(halo + low, halo + low + block)
        dq_ref[:, mine] = turn(dq, cosine[:, own_seen], -sine[:, own_seen]).astype(BF)
    dk = turn(dk_sum[...] * scale, cosine, -sine).astype(BF)
    dk_ref[...] = dk[:, halo:]
    edge_ref[:, :MOST] = dk[:, halo - MOST : halo]
    dv = dv_sum[...].astype(BF)
    dv_ref[...] = dv[:, halo:]
    edge_ref[:, MOST:] = dv[:, halo - MOST : halo]


def attend_back(q, k, v, g, logs, cosine, sine, begin, halo, block, first, heads):
    own = q.shape[1]
    total = halo + own
    inner = heads * HEAD_DIM
    per = lambda n: pl.BlockSpec((HEAD_DIM, n), lambda i: (first + i, 0))
    put = lambda n: pl.BlockSpec((HEAD_DIM, n), lambda i: (i, 0))
    full = lambda a: pl.BlockSpec(a.shape, lambda i: (0, 0))
    return pl.pallas_call(
        partial(attend_back_kernel, halo, block),
        grid=(heads,),
        out_shape=tuple(jax.ShapeDtypeStruct((inner, n), BF) for n in (own, own, own, 2 * MOST)),
        in_specs=[per(own), per(total), per(total), per(own), pl.BlockSpec((1, 1, own), lambda i: (i, 0, 0)),
                  full(cosine), full(sine), full(begin)],
        out_specs=tuple(put(n) for n in (own, own, own, 2 * MOST)),
        scratch_shapes=[
            pltpu.VMEM((own // block, halo + block, block), F32),
            pltpu.VMEM((HEAD_DIM, total), F32),
            pltpu.VMEM((HEAD_DIM, total), F32),
        ],
        compiler_params=pltpu.CompilerParams(vmem_limit_bytes=16 * MIB),
        name="attend_back",
        cost_estimate=work(2 * heads),
    )(q, k, v, g, logs, cosine, sine, begin)


def output_norm(weight, attended, x, gain, halo):
    width, total = x.shape
    own = total - halo

    def body(smem, ready, ins, outs, scratch):
        x_ref, gain_ref = ins
        resid_ref, second_ref, r_ref = outs
        att_ref, w_ref = ready(1), ready(0)

        def step(start, count):
            at = pl.ds(start, count)
            resid = dot_nn(w_ref[...], att_ref[:, at]) + x_ref[:, pl.ds(shifted(start, halo), count)].astype(F32)
            factor = lax.rsqrt(jnp.mean(resid * resid, axis=0, keepdims=True) + EPS)
            resid_ref[:, at] = resid
            r_ref[:, at] = factor
            second_ref[:, at] = (resid * factor * gain_ref[...]).astype(BF)

        over_tokens(own, step)

    return run(body, "output_norm", 6, 20, [((width, own), F32), ((width, own), BF), ((1, own), F32)],
               [weight, attended], [x, gain])


def forward_hidden(weight, second, shift, cot):
    width, own = second.shape
    root = math.sqrt(2.0 / math.pi)

    def body(smem, ready, ins, outs, scratch):
        second_ref, shift_ref, cot_ref = ins
        active_ref, slope_ref, keep_ref, send_ref = outs
        w_ref = ready(0)

        def step(start, count):
            at = pl.ds(start, count)
            h = dot_tn(w_ref[...], second_ref[:, at]) + shift_ref[...]
            square = h * h
            t = jnp.tanh(root * (h + 0.044715 * (square * h)))
            half = 0.5 * (1.0 + t)
            active_ref[:, at] = (h * half).astype(BF)
            slope_ref[:, at] = (half + 0.5 * h * (1.0 - t * t) * (root * (1.0 + 3.0 * 0.044715 * square))).astype(BF)

        over_tokens(own, step)
        gradient(cot_ref, slice(None), lambda: active_ref[...], keep_ref, send_ref)

    half = (width // 2, width)
    return run(body, "forward_hidden", 10, 24, [((width, own), BF), ((width, own), BF), (half, BF), (half, BF)],
               [weight], [second, shift, cot])


def back_project(weight, cot, slope, second):
    width, own = second.shape

    def body(smem, ready, ins, outs, scratch):
        cot_ref, slope_ref, second_ref = ins
        pre_ref, bias_ref, keep_ref, send_ref = outs
        (sums,) = scratch
        w_ref = ready(0)
        sums[...] = jnp.zeros_like(sums)

        def step(start, count):
            at = pl.ds(start, count)
            pre = (dot_tn(w_ref[...], cot_ref[:, at]) * slope_ref[:, at].astype(F32)).astype(BF)
            pre_ref[:, at] = pre
            sums[...] += lane_sums(pre.astype(F32))

        over_tokens(own, step)
        bias_ref[...] = jnp.sum(sums[...], axis=1, keepdims=True)
        gradient(second_ref, slice(None), lambda: pre_ref[...], keep_ref, send_ref)

    half = (width // 2, width)
    return run(body, "back_project", 9, 22, [((width, own), BF), ((width, 1), F32), (half, BF), (half, BF)],
               [weight], [cot, slope, second], [pltpu.VMEM((width, 128), F32)])


def norm_back(grad_norm, source, factor, gain):
    scaled = gain * grad_norm
    inner = jnp.mean(scaled * source, axis=0, keepdims=True)
    return factor * scaled - source * (factor * factor * factor * inner), grad_norm * source * factor


def back_hidden(weight, pre, resid, factor, gain, cot, attended):
    width, own = pre.shape

    def body(smem, ready, ins, outs, scratch):
        pre_ref, resid_ref, factor_ref, gain_ref, cot_ref = ins
        grad_ref, branch_ref, gain_out, keep_ref, send_ref = outs
        (sums,) = scratch
        w_ref = ready(0)
        sums[...] = jnp.zeros_like(sums)

        def step(start, count):
            at = pl.ds(start, count)
            grad_norm = dot_nn(w_ref[...], pre_ref[:, at])
            back, gained = norm_back(grad_norm, resid_ref[:, at], factor_ref[:, at], gain_ref[...])
            grad = cot_ref[:, at].astype(F32) + back
            grad_ref[:, at] = grad
            branch_ref[:, at] = grad.astype(BF)
            sums[...] += lane_sums(gained)

        over_tokens(own, step)
        gain_out[...] = jnp.sum(sums[...], axis=1, keepdims=True)
        att_ref = ready(1)
        gradient(branch_ref, slice(None), lambda: att_ref[...], keep_ref, send_ref)

    half = (width // 2, width)
    return run(body, "back_hidden", 10, 28,
               [((width, own), F32), ((width, own), BF), ((width, 1), F32), (half, BF), (half, BF)],
               [weight, attended], [pre, resid, factor, gain, cot], [pltpu.VMEM((width, 128), F32)])


def back_output(weight, branch):
    width, own = branch.shape

    def body(smem, ready, ins, outs, scratch):
        w_ref = ready(0)

        def step(start, count):
            at = pl.ds(start, count)
            outs[0][:, at] = dot_tn(w_ref[...], ins[0][:, at]).astype(BF)

        over_tokens(own, step)

    (out,) = run(body, "back_output", 4.5, 14, [((width, own), BF)], [weight], [branch])
    return out


def weight_gradient(a, d, edge, side, halo, name):
    width, total = a.shape
    own = total - halo
    half = (width // 2, width)

    def body(smem, ready, ins, outs, scratch):
        (a_ref,) = ins
        keep_ref, send_ref = outs[:2]
        d_ref = ready(0)
        if edge is not None:
            tail = slice(own - MOST, own)
            d_ref[:, tail] = (d_ref[:, tail].astype(F32) + ready(1)[:, side : side + MOST].astype(F32)).astype(BF)
            outs[2][...] = d_ref[...]
        gradient(a_ref, slice(halo, halo + own), lambda: d_ref[...], keep_ref, send_ref)

    outs = [(half, BF), (half, BF)] + ([] if edge is None else [((width, own), BF)])
    return run(body, name, 5, 18, outs, [d] + ([] if edge is None else [edge]), [a])


def write_rows(parts, source_ref, value, held, out_ref, start, count):
    size = value.shape[0] // parts
    for part in range(parts):
        held[pl.ds(pl.multiple_of(source_ref[part] * size, 8), size), :] = value[part * size : (part + 1) * size]
    out_ref[pl.ds(start, count), :] = held[...].T.astype(BF)


def mix(weight, active, resid, shift, source, parts):
    width, own = active.shape
    part = 256 if own % 256 == 0 else own

    def body(smem, ready, ins, outs, scratch):
        active_ref, resid_ref, shift_ref = ins
        w_ref = ready(0)

        def step(start, count):
            at = pl.ds(start, count)
            value = dot_nn(w_ref[...], active_ref[:, at]) + resid_ref[:, at] + shift_ref[...]
            write_rows(parts, smem[0], value, scratch[0], outs[0], start, count)

        over_tokens(own, step)

    (out,) = run(body, "mix", 7, 18, [((own, width), BF)], [weight], [active, resid, shift],
                 [pltpu.VMEM((width, part), F32)], [source])
    return out


def back_input(weights, d_query, grads, x, factor, gain, grad_resid, halo, source, parts):
    width, own = grads[0].shape
    part = 256 if own % 256 == 0 else own

    def body(smem, ready, ins, outs, scratch):
        x_ref, factor_ref, gain_ref, grad_ref = ins[2:]
        out_ref, gain_out = outs
        held, sums = scratch
        w_refs = [ready(w) for w in range(3)]
        d_refs = [ready(3), *ins[:2]]
        sums[...] = jnp.zeros_like(sums)

        def step(start, count):
            at, moved = pl.ds(start, count), pl.ds(shifted(start, halo), count)
            grad_norm = dot_nn(w_refs[0][...], d_refs[0][:, at])
            for w in (1, 2):
                grad_norm = grad_norm + dot_nn(w_refs[w][...], d_refs[w][:, at])
            back, gained = norm_back(grad_norm, x_ref[:, moved].astype(F32), factor_ref[:, moved], gain_ref[...])
            sums[...] += lane_sums(gained)
            write_rows(parts, smem[0], grad_ref[:, at] + back, held, out_ref, start, count)

        over_tokens(own, step)
        gain_out[...] = jnp.sum(sums[...], axis=1, keepdims=True)

    return run(body, "back_input", 18, 36, [((own, width), BF), ((width, 1), F32)],
               [*weights, d_query], [*grads, x, factor, gain, grad_resid],
               [pltpu.VMEM((width, part), F32), pltpu.VMEM((width, 128), F32)], [source])


def local(fsdp, heads, tokens, w_query, w_key, w_value, w_output, w_hidden, bias_hidden, w_project,
          bias_output, gain_first, gain_second, lengths, cotangent):
    links = Links(fsdp, heads, w_query.shape[0])
    own, width = tokens.shape
    inner = w_query.shape[1] * heads
    f_at, h_at = lax.axis_index("fsdp"), lax.axis_index("heads")
    me = f_at * heads + h_at
    halo = 128 if own % 128 == 0 else MOST
    block = 256 if own % 256 == 0 else own
    source = f_at ^ reverse_bits(jnp.arange(fsdp, dtype=jnp.int32), links.fbits)
    back = reverse_bits(jnp.arange(fsdp, dtype=jnp.int32) ^ f_at, links.fbits)
    inner_source = h_at ^ reverse_bits(jnp.arange(heads, dtype=jnp.int32), links.hbits)
    inner_back = reverse_bits(jnp.arange(heads, dtype=jnp.int32) ^ h_at, links.hbits)

    piece = bias_hidden.shape[0]
    one = [[(0, 0)], [(0, 0)]]
    pair = lambda left, right: jnp.stack([left, right])[:, None]
    small = jnp.concatenate([bias_hidden, bias_output, gain_first, gain_second])[None]
    slots = links.y + [links.x, links.core] + links.z[::-1]
    lead = Lane(links.spread(pair(w_query, w_key), one, links.z))
    small = Lane(links.collect(small, slots))
    value = Lane(links.spread(w_value[None, None], one[:1], [links.x] + links.z))
    before = lax.ppermute(tokens[own - MOST :], "heads", [(i, i + 1) for i in range(heads - 1)])
    seen = jnp.concatenate([jnp.zeros((halo - MOST, width), tokens.dtype), before, tokens], axis=0)
    last = Lane(links.spread(pair(w_hidden, w_project.T), one, links.y[:1]))

    ends = jnp.cumsum(lengths, axis=1, dtype=jnp.int32)
    place = jnp.arange(ROW, dtype=jnp.int32)
    done = ends[:, None, :] <= place[None, :, None]
    offset = jnp.sum(jnp.where(done, lengths[:, None, :], 0), axis=2, dtype=jnp.int32)
    spot = (place[None] - offset).reshape(-1)
    spot = jnp.concatenate([jnp.zeros((halo,), jnp.int32), spot])
    spot = lax.dynamic_slice_in_dim(spot, h_at * own, halo + own, 0)
    begin = (jnp.arange(own, dtype=jnp.int32) + halo - spot[halo:])[None]
    half = HEAD_DIM // 2
    freq = jnp.exp(-jnp.arange(half, dtype=F32) * (2.0 * math.log(THETA) / HEAD_DIM))
    angle = freq[:, None] * spot.astype(F32)[None]
    cosine, sine = jnp.cos(angle), jnp.sin(angle)

    cot, grad_output_bias = flip_sum(cotangent, source, fsdp)
    tick([lead, small, value])
    while lead.open:
        tick([lead, small])
    both, places = lead.result
    query = Lane(links.plane(both[0], places[0], [links.x] + links.y))
    key = Lane(links.plane(both[1], places[1], links.y + [links.x]))
    (o_shard,) = tick([value, small, last], [w_output.T])
    output = Lane(links.spread(o_shard[None, None], one[:1], links.z))
    (both, places), last = finish(last), None
    tick([query, key])
    while value.open:
        tick([value, small])
    value = Lane(links.plane(value.result[0][0], value.result[1][0], links.y))
    (both,) = tick([output, small], [both])
    hidden = Lane(links.spread(both[:1], places[:1], links.z))
    small = finish(small)
    index = jnp.arange(fsdp * heads, dtype=jnp.int32)
    where = jnp.zeros_like(index)
    for i, bit in enumerate(slots):
        where = where | ((((index ^ me) >> bit) & 1) << i)
    small = small[where].astype(F32)
    small = small.reshape(fsdp, heads, 4, piece).transpose(2, 1, 0, 3).reshape(4, -1)

    def to_rel(vector):
        return vector.reshape(fsdp, -1)[source].reshape(-1, 1)

    shift_hidden = small[0].reshape(heads, -1)[inner_source].reshape(-1, 1)
    shift_output, gain_one, gain_two = to_rel(small[1]), to_rel(small[2]), to_rel(small[3])

    x, normed, factor_one = flip_norm(seen, source, gain_one, fsdp)
    while output.open:
        tick([output, query, key])
    output = Lane(links.plane(output.result[0][0], output.result[1][0], [links.x] + links.y))
    query, key = finish(query), finish(key)
    (normed, both) = tick([hidden], [normed, both])
    project_ = Lane(links.spread(both[1:], places[1:], links.z))
    q = project(query, normed, halo, cosine, sine, "queries")
    while hidden.open:
        tick([hidden], [])
    hidden = Lane(links.plane(hidden.result[0][0], hidden.result[1][0], links.y[1:] + [links.x]))
    (normed, q) = tick([value, output], [normed, q])
    k = project(key, normed, 0, cosine, sine, "keys")
    (normed, k) = tick([project_], [normed, k])
    value = finish(value)
    v = project(value, normed, 0, None, None, "values")
    count = inner // HEAD_DIM
    each = max(1, count // 2)
    attended, logs = [], []
    (v,) = tick([], [v])
    for first in range(0, count, each):
        out, log = attend(q, k, v, begin, halo, block, first, each)
        attended.append((out[None], [(first * HEAD_DIM, 0)]))
        logs.append(log)
        if first == 0:
            while project_.open:
                tick([project_])
            (v,) = tick([], [v, out])[:1]
            project_ = Lane(links.plane(project_.result[0][0], project_.result[1][0], links.y[1:] + [links.x]))
    logs = jnp.concatenate(logs, axis=0)
    (x,) = tick([output, hidden], [x, logs])[:1]
    output = finish(output)
    resid, second, factor_two = output_norm(output, attended, x, gain_two, halo)
    (second,) = tick([hidden, project_], [second])
    hidden = finish(hidden)
    active, slope, keep, send = forward_hidden(hidden, second, shift_hidden, cot)
    fold_p = Lane(links.fold_plane(keep, send, "y"))
    (slope,) = tick([project_], [slope])
    project_ = finish(project_)
    grad_pre, grad_hidden_bias, keep, send = back_project(project_, cot, slope, second)
    fold_h = Lane(links.fold_plane(keep, send, "x"))
    (grad_pre,) = tick([fold_p], [grad_pre])
    grad_resid, branch, grad_gain_second, keep, send = back_hidden(
        hidden, grad_pre, resid, factor_two, gain_two, cot, attended)
    fold_o = Lane(links.fold_plane(keep, send, "y"))
    (branch,) = tick([fold_h], [branch])
    gradient_in = back_output(output, branch)

    parts = []
    count = inner // HEAD_DIM
    each = max(1, count // 4)
    plan = [[fold_o], [fold_p], [fold_h], [fold_o, fold_p]]
    for n, first in enumerate(range(0, count, each)):
        waits = plan[n] if n < len(plan) else []
        (gradient_in, *_) = tick(waits, [gradient_in] + [part[0] for part in parts[-1:]])
        parts.append(attend_back(q, k, v, gradient_in, logs[first : first + each], cosine, sine, begin, halo, block, first, each))
    spots = [[(first * HEAD_DIM, 0)] for first in range(0, count, each)]
    edge = jnp.concatenate([part[3] for part in parts], axis=0)
    edge = lax.ppermute(edge, "heads", [(i + 1, i) for i in range(heads - 1)]).reshape(heads, -1, 2 * MOST)
    step = inner // heads
    if heads == 2:
        edge = [(edge, [(step, 0), (0, 0)])]
    else:
        shuffle = reverse_bits((h_at + 1) ^ h_at, links.hbits) ^ jnp.arange(heads, dtype=jnp.int32)
        edge = [(edge[shuffle], [(step * i, 0) for i in range(heads)])]
    dq, dk, dv = ([(part[n][None], spot) for part, spot in zip(parts, spots)] for n in range(3))
    (normed,) = tick([fold_h, fold_o], [normed])
    keep, send = weight_gradient(normed, dq, None, 0, halo, "grad_query")
    fold_q = Lane(links.fold_plane(keep, send, "x"))
    front = Lane(links.fold_group([finish(fold_p), finish(fold_h), finish(fold_o)]))
    keep, send, dk = weight_gradient(normed, dk, edge, 0, halo, "grad_key")
    fold_k = Lane(links.fold_plane(keep, send, "y"))
    (normed, dk) = tick([fold_q], [normed, dk])
    keep, send, dv = weight_gradient(normed, dv, edge, MOST, halo, "grad_value")
    fold_v = Lane(links.fold_plane(keep, send, "y"))
    (dv,) = tick([fold_k, front], [dv])
    (dv,) = tick([fold_v], [dv])
    grad_tokens, grad_gain_first = back_input(
        [query, key, value], dq, [dk, dv], x, factor_one, gain_one, grad_resid, halo, source, fsdp)
    (active, _) = tick([fold_q, fold_k, front], [active, grad_gain_first])
    mixed = mix(project_, active, resid, shift_output, source, fsdp)
    out_project, out_hidden, out_output = finish(front)
    tick([fold_v, fold_q, fold_k], [mixed])
    pair_qk = Lane(links.fold_group([finish(fold_q), finish(fold_k)]))
    tick([pair_qk])
    single_v = Lane(links.fold_group([finish(fold_v)]))
    (out_query, out_key), (out_value,) = finish(pair_qk), finish(single_v)

    def to_abs(vector):
        return vector.reshape(fsdp, -1)[back].reshape(-1)

    vecs = jnp.stack([
        grad_hidden_bias.reshape(heads, -1)[inner_back].reshape(-1),
        to_abs(grad_output_bias), to_abs(grad_gain_first), to_abs(grad_gain_second),
    ])
    vecs = vecs.reshape(4, heads, fsdp, piece).transpose(2, 1, 0, 3).reshape(fsdp * heads, 4 * piece)
    vecs = vecs[me ^ jnp.arange(fsdp * heads, dtype=jnp.int32)]
    for bit in reversed(range(links.hbits + links.fbits)):
        rows = vecs.shape[0] // 2
        vecs = vecs[:rows] + links.swap(vecs[rows:], bit)
    vecs = vecs.reshape(4, piece)

    return (
        mixed, grad_tokens,
        out_query, out_key, out_value, out_output.T, out_hidden,
        vecs[0], out_project.T, vecs[1], vecs[2], vecs[3],
    )


def solution(mesh):
    fsdp, heads = mesh.shape["fsdp"], mesh.shape["heads"]
    rows, cols = P("fsdp", "heads"), P("heads", "fsdp")
    tokens, vector = P(("fsdp", "heads"), None), P(("heads", "fsdp"))
    return jax.shard_map(
        partial(local, fsdp, heads),
        mesh=mesh,
        in_specs=(tokens, rows, rows, rows, cols, rows, vector, cols, vector, vector, vector, P("fsdp", None), tokens),
        out_specs=(tokens, tokens, rows, rows, rows, cols, rows, vector, cols, vector, vector, vector),
        check_vma=False,
    )
```

```python
from functools import partial
import math

import jax
import jax.numpy as jnp
from jax import lax
from jax.experimental import pallas as pl
from jax.experimental.pallas import tpu as pltpu
from jax.sharding import PartitionSpec as P

HEAD_DIM = 80
ROW = 512
MOST = 64
EPS = 1e-06
NEG = -1e30
THETA = 10000.0
ALL = ("fsdp", "heads")
BF = jnp.bfloat16
F32 = jnp.float32
MIB = 1024 * 1024
TAIL = ("grad_query", "grad_key", "grad_value", "back_query", "back_key", "back_input", "mix")
PIN = False


def bits_of(n):
    return n.bit_length() - 1


def reverse_bits(values, count):
    out = 0
    for bit in range(count):
        out = out | (((values >> bit) & 1) << (count - 1 - bit))
    return out


class Lane:
    def __init__(self, steps):
        self.steps, self.result, self.pending = steps, None, []
        self.push(None)

    def push(self, values):
        try:
            self.pending = list(self.steps.send(values))
        except StopIteration as stop:
            self.steps, self.pending, self.result = None, [], stop.value

    @property
    def open(self):
        return self.steps is not None


def tick(lanes, values=()):
    lanes = [lane for lane in lanes if lane.open]
    counts = [len(lane.pending) for lane in lanes]
    flat = [v for lane in lanes for v in lane.pending] + list(values)
    flat = list(lax.optimization_barrier(tuple(flat)))
    at = 0
    for lane, count in zip(lanes, counts):
        lane.push(flat[at : at + count])
        at += count
    return flat[at:]


def finish(lane):
    while lane.open:
        tick([lane])
    return lane.result


class Links:
    def __init__(self, fsdp, heads, rows):
        self.count = fsdp * heads
        self.hbits, self.fbits = bits_of(heads), bits_of(fsdp)
        desc = list(range(self.hbits + self.fbits - 1, self.hbits - 1, -1))
        self.z, self.x, self.core = desc[:-2], desc[-2], desc[-1]
        self.y = list(range(self.hbits - 1, -1, -1))
        self.shift = {bit: (rows << i, 0) for i, bit in enumerate(desc)}
        self.shift.update({bit: (0, 1 << i) for i, bit in enumerate(self.y)})

    def swap(self, value, bit):
        pairs = [(d, d ^ (1 << bit)) for d in range(self.count)]
        return lax.ppermute(value, ALL, pairs)

    def moved(self, places, bit):
        row, group = self.shift[bit]
        return [(r + row, g + group) for r, g in places]

    def spread(self, value, places, bits):
        for bit in bits:
            value, other = yield [value, self.swap(value, bit)]
            value = jnp.concatenate([value, other], axis=1)
            places = [p + self.moved(p, bit) for p in places]
        return value, places

    def plane(self, value, places, bits):
        for bit in bits[:-1]:
            value, other = yield [value, self.swap(value, bit)]
            value = jnp.concatenate([value, other], axis=0)
            places = places + self.moved(places, bit)
        value, other, far = yield [value, self.swap(value, bits[-1]), self.swap(value, self.core)]
        last = self.moved(places, bits[-1])
        far_other = self.swap(other, self.core)
        pieces = [(value, places), (other, last), (far, self.moved(places, self.core)),
                  (far_other, self.moved(last, self.core))]
        pieces = [self.packed(v, p) for v, p in pieces]
        if value.shape[2] % 128:
            return self.whole(pieces)
        return pieces

    def packed(self, value, places):
        n, rows, cols = value.shape
        run = 1
        while run * 2 <= n and all(
            places[i + j] == (places[i][0] + j * rows, places[i][1])
            for i in range(0, n, run * 2) for j in range(run * 2)
        ):
            run *= 2
        return value.reshape(n // run, rows * run, cols), places[::run]

    def whole(self, pieces):
        cols = pieces[0][0].shape[2]
        rows = max(r + v.shape[1] for v, places in pieces for r, g in places)
        groups = max(g + 1 for v, places in pieces for r, g in places)
        full = jnp.zeros((rows, groups * cols), BF)
        for v, places in pieces:
            for i, (r, g) in enumerate(places):
                full = lax.dynamic_update_slice(full, v[i], (r, g * cols))
        return [(full[None], [(0, 0)])]

    def halves(self, value, axis):
        half = value.shape[axis] // 2
        return (lax.slice_in_dim(value, 0, half, axis=axis), lax.slice_in_dim(value, half, 2 * half, axis=axis))

    def add(self, keep, received):
        return (keep.astype(F32) + received.astype(F32)).astype(BF)

    def fold_plane(self, keep, send, first):
        keep, received = yield [keep, self.swap(send, self.core)]
        value = self.add(keep, received)
        steps = [(self.x, 0)] + [(b, 1) for b in reversed(self.y)]
        if first == "y":
            steps = steps[1:] + steps[:1]
        for bit, axis in steps:
            keep, send = self.halves(value, axis)
            keep, received = yield [keep, self.swap(send, bit)]
            value = self.add(keep, received)
        return value

    def fold(self, keep, send, order):
        keep, received = yield [keep, self.swap(send, self.core)]
        value = self.add(keep, received)
        left = [self.x] + self.z[::-1]
        for bit in order:
            if bit in self.y:
                keep, send = self.halves(value, 1)
            else:
                outer = 1 << left.index(bit)
                left.remove(bit)
                value = value.reshape(outer, 2, -1, value.shape[-1])
                keep, send = (value[:, i].reshape(-1, value.shape[-1]) for i in range(2))
            keep, received = yield [keep, self.swap(send, bit)]
            value = self.add(keep, received)
        return value.astype(F32)

    def fold_small(self, rows):
        for bit in sorted(self.shift, reverse=True):
            half = rows.shape[0] // 2
            keep, received = yield [rows[:half], self.swap(rows[half:], bit)]
            rows = keep + received
        return rows

    def fold_group(self, values):
        both = jnp.stack(values)
        for bit in reversed(self.z):
            keep, send = self.halves(both, 1)
            keep, received = yield [keep, self.swap(send, bit)]
            both = self.add(keep, received)
        return [both[i].astype(F32) for i in range(len(values))]

    def collect(self, value, bits):
        for bit in bits:
            value, other = yield [value, self.swap(value, bit)]
            value = jnp.concatenate([value, other], axis=0)
        return value


def pinned(value):
    return pltpu.with_memory_space_constraint(value, pltpu.HBM) if PIN else value


def work(us):
    return pl.CostEstimate(flops=int(us * 0.55e9), bytes_accessed=1 << 20, transcendentals=0)


def dot_tn(left, right):
    return lax.dot_general(left, right, (((0,), (0,)), ((), ())), preferred_element_type=F32)


def dot_nn(left, right):
    return lax.dot_general(left, right, (((1,), (0,)), ((), ())), preferred_element_type=F32)


def dot_nt(left, right):
    return lax.dot_general(left, right, (((1,), (1,)), ((), ())), preferred_element_type=F32)


class Column:
    def __init__(self, row):
        self.row = row


def row_sums(sums):
    return jnp.sum(sums.T, axis=0, keepdims=True)


def run(body, name, us, mib, outs, weights, args, scratch=(), smem=()):
    plans = [[places for _, places in pieces] for pieces in weights]
    arrays = [v for pieces in weights for v, _ in pieces]
    copies = [sum(v.shape[0] for v, _ in pieces) for pieces in weights]
    shapes = []
    for pieces in weights:
        rows = max(r + v.shape[1] for v, places in pieces for r, g in places)
        groups = max(g + 1 for v, places in pieces for r, g in places)
        shapes.append((rows, groups * pieces[0][0].shape[2]))
    turned = [i for i, arg in enumerate(args) if isinstance(arg, Column)]
    args = [arg.row if isinstance(arg, Column) else arg for arg in args]
    scratch = [pltpu.VMEM((args[i].shape[1], 1), F32) for i in turned] + list(scratch)
    n_s, n_a, n_in, n_w, n_out = len(smem), len(arrays), len(args), len(weights), len(outs)

    def kernel(*refs):
        at = 0
        s_refs, at = refs[at : at + n_s], at + n_s
        a_refs, at = refs[at : at + n_a], at + n_a
        in_refs, at = refs[at : at + n_in], at + n_in
        o_refs, at = refs[at : at + n_out], at + n_out
        w_refs, at = refs[at : at + n_w], at + n_w
        sems, at = refs[at : at + n_w], at + n_w
        started = []
        k = 0
        for w, plan in enumerate(plans):
            n = 0
            mine = []
            for places in plan:
                piece = a_refs[k]
                k += 1
                _, rows, cols = piece.shape
                for i, (row, group) in enumerate(places):
                    target = w_refs[w].at[row : row + rows, group * cols : (group + 1) * cols]
                    mine.append(pltpu.make_async_copy(piece.at[i], target, sems[w].at[n]))
                    n += 1
            started.append(mine)
        for mine in started:
            for copy in mine:
                copy.start()

        def ready(w):
            for copy in started[w]:
                copy.wait()
            return w_refs[w]

        in_refs = list(in_refs)
        for i in turned:
            row = in_refs[i][...]
            refs[at][...] = jnp.broadcast_to(row, (128, row.shape[1])).T[:, :1]
            in_refs[i], at = refs[at], at + 1
        body(s_refs, ready, in_refs, o_refs, refs[at:])

    vmem, anywhere = pl.BlockSpec(memory_space=pltpu.VMEM), pl.BlockSpec(memory_space=pl.ANY)
    out = pl.pallas_call(
        kernel,
        name=name,
        out_shape=tuple(jax.ShapeDtypeStruct(s, d) for s, d in outs),
        in_specs=[pl.BlockSpec(memory_space=pltpu.SMEM)] * n_s + [anywhere] * n_a + [vmem] * n_in,
        out_specs=(vmem,) * n_out,
        scratch_shapes=[pltpu.VMEM(s, BF) for s in shapes]
        + [pltpu.SemaphoreType.DMA((n,)) for n in copies] + list(scratch),
        compiler_params=pltpu.CompilerParams(vmem_limit_bytes=mib * MIB),
        cost_estimate=work(us * (0.3 if name in TAIL else 1)),
    )(*smem, *arrays, *args)
    return out


def over_tokens(own, step):
    part = 256 if own % 256 == 0 else own
    if part == own:
        step(0, own)
        return

    @pl.loop(0, own // part)
    def _(i):
        step(pl.multiple_of(i * part, part), part)


def shifted(start, by):
    return start + by if isinstance(start, int) else pl.multiple_of(start + by, 128)


def lane_sums(value):
    count = value.shape[1]
    if count % 128:
        return jnp.pad(jnp.sum(value, axis=1, keepdims=True), ((0, 0), (0, 127)))
    out = value[:, :128]
    for i in range(1, count // 128):
        out = out + value[:, i * 128 : (i + 1) * 128]
    return out


def gradient(left_ref, lanes, right, keep_ref, send_ref):
    rows = keep_ref.shape[0]
    part = 320 if rows % 320 == 0 else rows

    for first, out_ref in ((rows, send_ref), (0, keep_ref)):
        @pl.loop(0, rows // part)
        def _(i):
            at = pl.multiple_of(first + i * part, 16)
            value = dot_nt(left_ref[pl.ds(at, part), lanes], right())
            out_ref[pl.ds(pl.multiple_of(i * part, 16), part), :] = value.astype(BF)


def flip_rows(parts, source, held, put):
    size = held.shape[0] // parts
    for part in range(parts):
        start = pl.multiple_of(source[part] * size, 8)
        put(part * size, size, start)


def flip_norm(seen, source, gain, parts):
    tokens, width = seen.shape

    def body(smem, ready, ins, outs, scratch):
        (source_ref,), (seen_ref, gain_ref), (x_ref, a_ref, r_ref), (held, moved) = smem, ins, outs, scratch
        held[...] = seen_ref[...].astype(F32).T

        def put(row, size, start):
            moved[row : row + size, :] = held[pl.ds(start, size), :]

        flip_rows(parts, source_ref, held, put)
        x = moved[...]
        factor = lax.rsqrt(jnp.mean(x * x, axis=0, keepdims=True) + EPS)
        x_ref[...] = x.astype(BF)
        r_ref[...] = factor
        a_ref[...] = (x * factor * gain_ref[...]).astype(BF)

    return run(body, "flip_norm", 9, 24, [((width, tokens), BF), ((width, tokens), BF), ((1, tokens), F32)],
               [], [seen, Column(gain)], [pltpu.VMEM((width, tokens), F32)] * 2, [source])


def flip_sum(value, source, parts):
    tokens, width = value.shape

    def body(smem, ready, ins, outs, scratch):
        (source_ref,), (value_ref,), (x_ref, sum_ref), (held, moved) = smem, ins, outs, scratch
        held[...] = value_ref[...].astype(F32).T

        def put(row, size, start):
            moved[row : row + size, :] = held[pl.ds(start, size), :]

        flip_rows(parts, source_ref, held, put)
        x_ref[...] = moved[...].astype(BF)
        sum_ref[...] = row_sums(lane_sums(moved[...]))

    return run(body, "flip_sum", 6, 20, [((width, tokens), BF), ((1, width), F32)],
               [], [value], [pltpu.VMEM((width, tokens), F32)] * 2, [source])


def turn(vectors, cosine, sine):
    half = vectors.shape[0] // 2
    first, second = vectors[:half], vectors[half:]
    return jnp.concatenate([first * cosine - second * sine, second * cosine + first * sine], axis=0)


def project(weight, a, low, cosine, sine, name):
    width, total = a.shape
    inner = width
    own = total - low if low else None

    def body(smem, ready, ins, outs, scratch):
        (out_ref,) = outs
        a_ref = ins[0]
        w_ref = ready(0)

        def step(start, count, goes):
            value = dot_tn(w_ref[...], a_ref[:, pl.ds(start, count)])
            if cosine is None:
                out_ref[:, pl.ds(goes, count)] = value.astype(BF)
                return
            c, s = ins[1][:, pl.ds(start, count)], ins[2][:, pl.ds(start, count)]
            for head in range(inner // HEAD_DIM):
                rows = slice(head * HEAD_DIM, (head + 1) * HEAD_DIM)
                out_ref[rows, pl.ds(goes, count)] = turn(value[rows], c, s).astype(BF)

        if low:
            over_tokens(own, lambda start, count: step(shifted(start, low), count, start))
        elif total % 256 == 128:
            step(0, 128, 0)
            over_tokens(total - 128, lambda start, count: step(shifted(start, 128), count, shifted(start, 128)))
        else:
            step(0, total, 0)

    args = [a] if cosine is None else [a, cosine, sine]
    (out,) = run(body, name, 5, 18, [((inner, total - low), BF)], [weight], args)
    return out


def fill_bias(begin_ref, bias_ref, halo, block, window):
    for b in range(bias_ref.shape[0]):
        low = b * block
        key = lax.broadcasted_iota(jnp.int32, (window, block), 0) + low
        query = lax.broadcasted_iota(jnp.int32, (window, block), 1) + (halo + low)
        begin = begin_ref[0:1, low : low + block]
        bias_ref[b] = jnp.where((key >= begin) & (key <= query), 0.0, NEG)


def attend_kernel(halo, block, q_ref, k_ref, v_ref, begin_ref, att_ref, log_ref, bias_ref):
    own = q_ref.shape[1]
    window = halo + block
    scale = HEAD_DIM ** (-0.5)

    @pl.when(pl.program_id(0) == 0)
    def _():
        fill_bias(begin_ref, bias_ref, halo, block, window)

    for b in range(own // block):
        low = b * block
        mine, seen = slice(low, low + block), slice(low, low + window)
        scores = dot_tn(k_ref[:, seen], q_ref[:, mine]) * scale + bias_ref[b]
        peak = jnp.max(scores, axis=0, keepdims=True)
        expo = jnp.exp(scores - peak)
        total = jnp.sum(expo, axis=0, keepdims=True)
        weights = (expo * (1.0 / total)).astype(BF)
        att_ref[:, mine] = dot_nn(v_ref[:, seen], weights).astype(BF)
        log_ref[0, :, mine] = peak + jnp.log(total)


def attend(q, k, v, begin, halo, block, first, heads):
    own = q.shape[1]
    total = halo + own
    inner = heads * HEAD_DIM
    per = lambda n: pl.BlockSpec((HEAD_DIM, n), lambda i: (first + i, 0))
    put = pl.BlockSpec((HEAD_DIM, own), lambda i: (i, 0))
    return pl.pallas_call(
        partial(attend_kernel, halo, block),
        grid=(heads,),
        out_shape=(jax.ShapeDtypeStruct((inner, own), BF), jax.ShapeDtypeStruct((heads, 1, own), F32)),
        in_specs=[per(own), per(total), per(total), pl.BlockSpec(begin.shape, lambda i: (0, 0))],
        out_specs=(put, pl.BlockSpec((1, 1, own), lambda i: (i, 0, 0))),
        scratch_shapes=[pltpu.VMEM((own // block, halo + block, block), F32)],
        compiler_params=pltpu.CompilerParams(vmem_limit_bytes=12 * MIB),
        name="attend",
        cost_estimate=work(1.2 * heads),
    )(q, k, v, begin)


def attend_back_kernel(halo, block, q_ref, k_ref, v_ref, g_ref, log_ref, cos_ref, sin_ref, begin_ref,
                       dq_ref, dk_ref, dv_ref, edge_ref, bias_ref, dk_sum, dv_sum):
    own = q_ref.shape[1]
    window = halo + block
    scale = HEAD_DIM ** (-0.5)

    @pl.when(pl.program_id(0) == 0)
    def _():
        fill_bias(begin_ref, bias_ref, halo, block, window)

    cosine, sine = cos_ref[...], sin_ref[...]
    dk_sum[...] = jnp.zeros_like(dk_sum)
    dv_sum[...] = jnp.zeros_like(dv_sum)
    for b in range(own // block):
        low = b * block
        mine, seen = slice(low, low + block), slice(low, low + window)
        qb, kb, vb, gb = q_ref[:, mine], k_ref[:, seen], v_ref[:, seen], g_ref[:, mine]
        scores = dot_tn(kb, qb) * scale + bias_ref[b]
        probs = jnp.exp(scores - log_ref[0, :, mine])
        dv_sum[:, seen] += dot_nt(gb, probs.astype(BF))
        grad_probs = dot_tn(vb, gb)
        inner = jnp.sum(probs * grad_probs, axis=0, keepdims=True)
        grad_scores = (probs * (grad_probs - inner)).astype(BF)
        dq = dot_nn(kb, grad_scores) * scale
        dk_sum[:, seen] += dot_nt(qb, grad_scores)
        own_seen = slice(halo + low, halo + low + block)
        dq_ref[:, mine] = turn(dq, cosine[:, own_seen], -sine[:, own_seen]).astype(BF)
    dk = turn(dk_sum[...] * scale, cosine, -sine).astype(BF)
    dk_ref[...] = dk[:, halo:]
    edge_ref[:, :MOST] = dk[:, halo - MOST : halo]
    dv = dv_sum[...].astype(BF)
    dv_ref[...] = dv[:, halo:]
    edge_ref[:, MOST:] = dv[:, halo - MOST : halo]


def attend_back(q, k, v, g, logs, cosine, sine, begin, halo, block, first, heads):
    own = q.shape[1]
    total = halo + own
    inner = heads * HEAD_DIM
    per = lambda n: pl.BlockSpec((HEAD_DIM, n), lambda i: (first + i, 0))
    put = lambda n: pl.BlockSpec((HEAD_DIM, n), lambda i: (i, 0))
    full = lambda a: pl.BlockSpec(a.shape, lambda i: (0, 0))
    return pl.pallas_call(
        partial(attend_back_kernel, halo, block),
        grid=(heads,),
        out_shape=tuple(jax.ShapeDtypeStruct((inner, n), BF) for n in (own, own, own, 2 * MOST)),
        in_specs=[per(own), per(total), per(total), per(own), pl.BlockSpec((1, 1, own), lambda i: (i, 0, 0)),
                  full(cosine), full(sine), full(begin)],
        out_specs=tuple(put(n) for n in (own, own, own, 2 * MOST)),
        scratch_shapes=[
            pltpu.VMEM((own // block, halo + block, block), F32),
            pltpu.VMEM((HEAD_DIM, total), F32),
            pltpu.VMEM((HEAD_DIM, total), F32),
        ],
        compiler_params=pltpu.CompilerParams(vmem_limit_bytes=16 * MIB),
        name="attend_back",
        cost_estimate=work(2 * heads),
    )(q, k, v, g, logs, cosine, sine, begin)


def output_norm(weight, attended, x, gain, halo):
    width, total = x.shape
    own = total - halo

    def body(smem, ready, ins, outs, scratch):
        x_ref, gain_ref = ins
        resid_ref, second_ref, r_ref = outs
        att_ref, w_ref = ready(1), ready(0)

        def step(start, count):
            at = pl.ds(start, count)
            resid = dot_nn(w_ref[...], att_ref[:, at]) + x_ref[:, pl.ds(shifted(start, halo), count)].astype(F32)
            factor = lax.rsqrt(jnp.mean(resid * resid, axis=0, keepdims=True) + EPS)
            resid_ref[:, at] = resid
            r_ref[:, at] = factor
            second_ref[:, at] = (resid * factor * gain_ref[...]).astype(BF)

        over_tokens(own, step)

    return run(body, "output_norm", 6, 20, [((width, own), F32), ((width, own), BF), ((1, own), F32)],
               [weight, attended], [x, Column(gain)])


def forward_hidden(weight, second, shift, cot):
    width, own = second.shape
    root = math.sqrt(2.0 / math.pi)

    def body(smem, ready, ins, outs, scratch):
        second_ref, shift_ref, cot_ref = ins
        active_ref, slope_ref, keep_ref, send_ref = outs
        w_ref = ready(0)

        def step(start, count):
            at = pl.ds(start, count)
            h = dot_tn(w_ref[...], second_ref[:, at]) + shift_ref[...]
            square = h * h
            t = jnp.tanh(root * (h + 0.044715 * (square * h)))
            half = 0.5 * (1.0 + t)
            active_ref[:, at] = (h * half).astype(BF)
            slope_ref[:, at] = (half + 0.5 * h * (1.0 - t * t) * (root * (1.0 + 3.0 * 0.044715 * square))).astype(BF)

        over_tokens(own, step)
        gradient(cot_ref, slice(None), lambda: active_ref[...], keep_ref, send_ref)

    half = (width // 2, width)
    return run(body, "forward_hidden", 10, 24, [((width, own), BF), ((width, own), BF), (half, BF), (half, BF)],
               [weight], [second, Column(shift), cot])


def back_project(weight, cot, slope, second):
    width, own = second.shape

    def body(smem, ready, ins, outs, scratch):
        cot_ref, slope_ref, second_ref = ins
        pre_ref, bias_ref, keep_ref, send_ref = outs
        (sums,) = scratch
        w_ref = ready(0)
        sums[...] = jnp.zeros_like(sums)

        def step(start, count):
            at = pl.ds(start, count)
            pre = (dot_tn(w_ref[...], cot_ref[:, at]) * slope_ref[:, at].astype(F32)).astype(BF)
            pre_ref[:, at] = pre
            sums[...] += lane_sums(pre.astype(F32))

        over_tokens(own, step)
        bias_ref[...] = row_sums(sums[...])
        gradient(second_ref, slice(None), lambda: pre_ref[...], keep_ref, send_ref)

    half = (width // 2, width)
    return run(body, "back_project", 9, 22, [((width, own), BF), ((1, width), F32), (half, BF), (half, BF)],
               [weight], [cot, slope, second], [pltpu.VMEM((width, 128), F32)])


def norm_back(grad_norm, source, factor, gain):
    scaled = gain * grad_norm
    inner = jnp.mean(scaled * source, axis=0, keepdims=True)
    return factor * scaled - source * (factor * factor * factor * inner), grad_norm * source * factor


def back_hidden(weight, pre, resid, factor, gain, cot, attended):
    width, own = pre.shape

    def body(smem, ready, ins, outs, scratch):
        pre_ref, resid_ref, factor_ref, gain_ref, cot_ref = ins
        grad_ref, branch_ref, gain_out, keep_ref, send_ref = outs
        (sums,) = scratch
        w_ref = ready(0)
        sums[...] = jnp.zeros_like(sums)

        def step(start, count):
            at = pl.ds(start, count)
            grad_norm = dot_nn(w_ref[...], pre_ref[:, at])
            back, gained = norm_back(grad_norm, resid_ref[:, at], factor_ref[:, at], gain_ref[...])
            grad = cot_ref[:, at].astype(F32) + back
            grad_ref[:, at] = grad
            branch_ref[:, at] = grad.astype(BF)
            sums[...] += lane_sums(gained)

        over_tokens(own, step)
        gain_out[...] = row_sums(sums[...])
        att_ref = ready(1)
        gradient(branch_ref, slice(None), lambda: att_ref[...], keep_ref, send_ref)

    half = (width // 2, width)
    return run(body, "back_hidden", 10, 28,
               [((width, own), F32), ((width, own), BF), ((1, width), F32), (half, BF), (half, BF)],
               [weight, attended], [pre, resid, factor, Column(gain), cot], [pltpu.VMEM((width, 128), F32)])


def back_output(weight, branch):
    width, own = branch.shape

    def body(smem, ready, ins, outs, scratch):
        w_ref = ready(0)

        def step(start, count):
            at = pl.ds(start, count)
            outs[0][:, at] = dot_tn(w_ref[...], ins[0][:, at]).astype(BF)

        over_tokens(own, step)

    (out,) = run(body, "back_output", 4.5, 14, [((width, own), BF)], [weight], [branch])
    return out


def weight_gradient(a, d, edge, side, halo, name):
    width, total = a.shape
    own = total - halo
    half = (width // 2, width)

    def body(smem, ready, ins, outs, scratch):
        (a_ref,) = ins
        keep_ref, send_ref = outs[:2]
        d_ref = ready(0)
        if edge is not None:
            tail = slice(own - MOST, own)
            d_ref[:, tail] = (d_ref[:, tail].astype(F32) + ready(1)[:, side : side + MOST].astype(F32)).astype(BF)
            outs[2][...] = d_ref[...]
        gradient(a_ref, slice(halo, halo + own), lambda: d_ref[...], keep_ref, send_ref)

    outs = [(half, BF), (half, BF)] + ([] if edge is None else [((width, own), BF)])
    return run(body, name, 5, 18, outs, [d] + ([] if edge is None else [edge]), [a])


def write_rows(parts, source_ref, value, held, out_ref, start, count):
    size = value.shape[0] // parts
    for part in range(parts):
        held[pl.ds(pl.multiple_of(source_ref[part] * size, 8), size), :] = value[part * size : (part + 1) * size]
    out_ref[pl.ds(start, count), :] = held[...].T.astype(BF)


def mix(weight, active, resid, shift, source, parts):
    width, own = active.shape
    part = 256 if own % 256 == 0 else own

    def body(smem, ready, ins, outs, scratch):
        active_ref, resid_ref, shift_ref = ins
        w_ref = ready(0)

        def step(start, count):
            at = pl.ds(start, count)
            value = dot_nn(w_ref[...], active_ref[:, at]) + resid_ref[:, at] + shift_ref[...]
            write_rows(parts, smem[0], value, scratch[0], outs[0], start, count)

        over_tokens(own, step)

    (out,) = run(body, "mix", 7, 18, [((own, width), BF)], [weight], [active, resid, Column(shift)],
                 [pltpu.VMEM((width, part), F32)], [source])
    return out


def back_part(weight, d, total, name):
    width = weight_rows(weight)
    own = d[0][0].shape[2]

    def body(smem, ready, ins, outs, scratch):
        d_ref, w_ref = ready(1), ready(0)

        def step(start, count):
            at = pl.ds(start, count)
            value = dot_nn(w_ref[...], d_ref[:, at])
            outs[0][:, at] = value if total is None else value + ins[0][:, at]

        over_tokens(own, step)

    (out,) = run(body, name, 5, 20, [((width, own), F32)], [weight, d], [] if total is None else [total])
    return out


def weight_rows(pieces):
    return max(r + v.shape[1] for v, places in pieces for r, g in places)


def back_input(weight, d, total, x, factor, gain, grad_resid, halo, source, parts):
    width, own = d.shape
    part = 256 if own % 256 == 0 else own

    def body(smem, ready, ins, outs, scratch):
        d_ref, total_ref, x_ref, factor_ref, gain_ref, grad_ref = ins
        out_ref, gain_out = outs
        held, sums = scratch
        w_ref = ready(0)
        sums[...] = jnp.zeros_like(sums)

        def step(start, count):
            at, moved = pl.ds(start, count), pl.ds(shifted(start, halo), count)
            grad_norm = dot_nn(w_ref[...], d_ref[:, at]) + total_ref[:, at]
            back, gained = norm_back(grad_norm, x_ref[:, moved].astype(F32), factor_ref[:, moved], gain_ref[...])
            sums[...] += lane_sums(gained)
            write_rows(parts, smem[0], grad_ref[:, at] + back, held, out_ref, start, count)

        over_tokens(own, step)
        gain_out[...] = row_sums(sums[...])

    return run(body, "back_input", 9, 32, [((own, width), BF), ((1, width), F32)],
               [weight], [d, total, x, factor, Column(gain), grad_resid],
               [pltpu.VMEM((width, part), F32), pltpu.VMEM((width, 128), F32)], [source])


def local(fsdp, heads, tokens, w_query, w_key, w_value, w_output, w_hidden, bias_hidden, w_project,
          bias_output, gain_first, gain_second, lengths, cotangent):
    links = Links(fsdp, heads, w_query.shape[0])
    own, width = tokens.shape
    inner = w_query.shape[1] * heads
    f_at, h_at = lax.axis_index("fsdp"), lax.axis_index("heads")
    me = f_at * heads + h_at
    halo = 128 if own % 128 == 0 else MOST
    block = 256 if own % 256 == 0 else own
    source = f_at ^ reverse_bits(jnp.arange(fsdp, dtype=jnp.int32), links.fbits)
    back = reverse_bits(jnp.arange(fsdp, dtype=jnp.int32) ^ f_at, links.fbits)
    inner_source = h_at ^ reverse_bits(jnp.arange(heads, dtype=jnp.int32), links.hbits)
    inner_back = reverse_bits(jnp.arange(heads, dtype=jnp.int32) ^ h_at, links.hbits)

    piece = bias_hidden.shape[0]
    one = [[(0, 0)], [(0, 0)]]
    pair = lambda left, right: jnp.stack([left, right])[:, None]
    small = jnp.concatenate([bias_hidden, bias_output, gain_first, gain_second])[None]
    slots = links.y + [links.x, links.core] + links.z[::-1]
    lead = Lane(links.spread(pair(w_query, w_key), one, links.z))
    small = Lane(links.collect(small, slots))
    value = Lane(links.spread(w_value[None, None], one[:1], [links.x] + links.z))
    before = lax.ppermute(tokens[own - MOST :], "heads", [(i, i + 1) for i in range(heads - 1)])
    seen = jnp.concatenate([jnp.zeros((halo - MOST, width), tokens.dtype), before, tokens], axis=0)
    last = Lane(links.spread(pair(w_hidden, w_project.T), one, links.y[:1]))

    ends = jnp.cumsum(lengths, axis=1, dtype=jnp.int32)
    place = jnp.arange(ROW, dtype=jnp.int32)
    done = ends[:, None, :] <= place[None, :, None]
    offset = jnp.sum(jnp.where(done, lengths[:, None, :], 0), axis=2, dtype=jnp.int32)
    spot = (place[None] - offset).reshape(-1)
    spot = jnp.concatenate([jnp.zeros((halo,), jnp.int32), spot])
    spot = lax.dynamic_slice_in_dim(spot, h_at * own, halo + own, 0)
    begin = (jnp.arange(own, dtype=jnp.int32) + halo - spot[halo:])[None]
    half = HEAD_DIM // 2
    freq = jnp.exp(-jnp.arange(half, dtype=F32) * (2.0 * math.log(THETA) / HEAD_DIM))
    angle = freq[:, None] * spot.astype(F32)[None]
    cosine, sine = jnp.cos(angle), jnp.sin(angle)

    cot, grad_output_bias = flip_sum(cotangent, source, fsdp)
    tick([lead, small, value])
    while lead.open:
        tick([lead, small])
    both, places = lead.result
    query = Lane(links.plane(both[0], places[0], [links.x] + links.y))
    key = Lane(links.plane(both[1], places[1], links.y + [links.x]))
    (o_shard,) = tick([value, small, last], [w_output.T])
    output = Lane(links.spread(o_shard[None, None], one[:1], links.z))
    (both, places), last = finish(last), None
    tick([query, key])
    while value.open:
        tick([value, small])
    value = Lane(links.plane(value.result[0][0], value.result[1][0], links.y))
    (both,) = tick([output, small], [both])
    hidden = Lane(links.spread(both[:1], places[:1], links.z))
    small = finish(small)
    index = jnp.arange(fsdp * heads, dtype=jnp.int32)
    where = jnp.zeros_like(index)
    for i, bit in enumerate(slots):
        where = where | ((((index ^ me) >> bit) & 1) << i)
    small = small[where].astype(F32)
    small = small.reshape(fsdp, heads, 4, piece).transpose(2, 1, 0, 3).reshape(4, -1)

    def to_rel(vector):
        return vector.reshape(fsdp, -1)[source].reshape(1, -1)

    shift_hidden = small[0].reshape(heads, -1)[inner_source].reshape(1, -1)
    shift_output, gain_one, gain_two = to_rel(small[1]), to_rel(small[2]), to_rel(small[3])

    x, normed, factor_one = flip_norm(seen, source, gain_one, fsdp)
    while output.open:
        tick([output, query, key])
    output = Lane(links.plane(output.result[0][0], output.result[1][0], [links.x] + links.y))
    query, key = finish(query), finish(key)
    (normed, both) = tick([hidden], [normed, both])
    project_ = Lane(links.spread(both[1:], places[1:], links.z))
    q = project(query, normed, halo, cosine, sine, "queries")
    while hidden.open:
        tick([hidden], [])
    hidden = Lane(links.plane(hidden.result[0][0], hidden.result[1][0], links.y[1:] + [links.x]))
    (normed, q) = tick([value, output], [normed, q])
    k = project(key, normed, 0, cosine, sine, "keys")
    (normed, k) = tick([project_], [normed, k])
    value = finish(value)
    v = project(value, normed, 0, None, None, "values")
    count = inner // HEAD_DIM
    each = max(1, count // 2)
    attended, logs = [], []
    (v,) = tick([], [v])
    for first in range(0, count, each):
        out, log = attend(q, k, v, begin, halo, block, first, each)
        attended.append((out[None], [(first * HEAD_DIM, 0)]))
        logs.append(log)
        if first == 0:
            while project_.open:
                tick([project_])
            (v,) = tick([], [v, out])[:1]
            project_ = Lane(links.plane(project_.result[0][0], project_.result[1][0], links.y[1:] + [links.x]))
    logs = jnp.concatenate(logs, axis=0)
    (x,) = tick([output, hidden], [x, logs])[:1]
    output = finish(output)
    resid, second, factor_two = output_norm(output, attended, x, gain_two, halo)
    (second,) = tick([hidden, project_], [second])
    hidden = finish(hidden)
    active, slope, keep, send = forward_hidden(hidden, second, shift_hidden, cot)
    fold_p = Lane(links.fold_plane(keep, send, "y"))
    (slope,) = tick([project_], [slope])
    project_ = finish(project_)
    grad_pre, grad_hidden_bias, keep, send = back_project(project_, cot, slope, second)
    fold_h = Lane(links.fold_plane(keep, send, "x"))
    (grad_pre,) = tick([fold_p], [grad_pre])
    grad_resid, branch, grad_gain_second, keep, send = back_hidden(
        hidden, grad_pre, resid, factor_two, gain_two, cot, attended)
    fold_o = Lane(links.fold_plane(keep, send, "y"))
    (branch,) = tick([fold_h], [branch])
    gradient_in = back_output(output, branch)

    parts = []
    count = inner // HEAD_DIM
    each = max(1, count // 4)
    plan = [[fold_o], [fold_p], [fold_h], [fold_o, fold_p]]
    for n, first in enumerate(range(0, count, each)):
        waits = plan[n] if n < len(plan) else []
        (gradient_in, *_) = tick(waits, [gradient_in] + [part[0] for part in parts[-1:]])
        parts.append(attend_back(q, k, v, gradient_in, logs[first : first + each], cosine, sine, begin, halo, block, first, each))
    spots = [[(first * HEAD_DIM, 0)] for first in range(0, count, each)]
    edge = jnp.concatenate([part[3] for part in parts], axis=0)
    edge = lax.ppermute(edge, "heads", [(i + 1, i) for i in range(heads - 1)]).reshape(heads, -1, 2 * MOST)
    step = inner // heads
    if heads == 2:
        edge = [(edge, [(step, 0), (0, 0)])]
    else:
        shuffle = reverse_bits((h_at + 1) ^ h_at, links.hbits) ^ jnp.arange(heads, dtype=jnp.int32)
        edge = [(edge[shuffle], [(step * i, 0) for i in range(heads)])]
    dq, dk, dv = ([(pinned(part[n])[None], spot) for part, spot in zip(parts, spots)] for n in range(3))
    up, down = links.y[::-1], links.z[::-1]
    (normed,) = tick([fold_h, fold_o], [normed])
    up, down = links.y[::-1], links.z[::-1]
    keep, send = weight_gradient(normed, dq, None, 0, halo, "grad_query")
    fold_q = Lane(links.fold(keep, send, [links.x] + up + down))
    front = Lane(links.fold_group([finish(fold_p), finish(fold_h), finish(fold_o)]))
    total = back_part(query, dq, None, "back_query")
    (normed, total) = tick([fold_q], [normed, total])
    keep, send, dk = weight_gradient(normed, dk, edge, 0, halo, "grad_key")
    fold_k = Lane(links.fold(keep, send, up + [links.x] + down))
    (normed, dk) = tick([front], [normed, dk])
    keep, send, dv = weight_gradient(normed, dv, edge, MOST, halo, "grad_value")
    fold_v = Lane(links.fold(keep, send, down[:1] + [links.x] + up + down[1:]))
    (total, dv) = tick([fold_k], [total, dv])
    total = back_part(key, [(dk[None], one[0])], total, "back_key")
    (total,) = tick([fold_v], [total])
    grad_tokens, grad_gain_first = back_input(
        value, dv, total, x, factor_one, gain_one, grad_resid, halo, source, fsdp)

    def to_abs(vector):
        return vector.reshape(fsdp, -1)[back].reshape(-1)

    vecs = jnp.stack([
        grad_hidden_bias.reshape(heads, -1)[inner_back].reshape(-1),
        to_abs(grad_output_bias), to_abs(grad_gain_first), to_abs(grad_gain_second),
    ])
    vecs = vecs.reshape(4, heads, fsdp, piece).transpose(2, 1, 0, 3).reshape(fsdp * heads, 4 * piece)
    vecs = Lane(links.fold_small(vecs[me ^ jnp.arange(fsdp * heads, dtype=jnp.int32)]))
    (active,) = tick([fold_q, front], [active, grad_gain_first])[:1]
    mixed = mix(project_, active, resid, shift_output, source, fsdp)
    tick([fold_v, fold_k, vecs], [mixed])
    tick([fold_q, vecs])
    tick([fold_v, fold_k, vecs])
    tick([fold_q, vecs])
    tick([fold_v, fold_k])
    out_query, out_key, out_value = finish(fold_q), finish(fold_k), finish(fold_v)
    vecs = finish(vecs)
    out_project, out_hidden, out_output = finish(front)
    vecs = vecs.reshape(4, piece)

    return (
        mixed, grad_tokens,
        out_query, out_key, out_value, out_output.T, out_hidden,
        vecs[0], out_project.T, vecs[1], vecs[2], vecs[3],
    )


def solution(mesh):
    fsdp, heads = mesh.shape["fsdp"], mesh.shape["heads"]
    rows, cols = P("fsdp", "heads"), P("heads", "fsdp")
    tokens, vector = P(("fsdp", "heads"), None), P(("heads", "fsdp"))
    return jax.shard_map(
        partial(local, fsdp, heads),
        mesh=mesh,
        in_specs=(tokens, rows, rows, rows, cols, rows, vector, cols, vector, vector, vector, P("fsdp", None), tokens),
        out_specs=(tokens, tokens, rows, rows, rows, cols, rows, vector, cols, vector, vector, vector),
        check_vma=False,
    )
```
